512 devices in a mesh: context: 64 (over z, y), tensor: 8 (over x, core).
Axes of the slice: x: 4, y: 8, z: 8, core: 2. Of those that a mesh axis runs over, the one named last changes fastest.
Arguments:
- query_proj: bfloat16 [8192, 8192], P('context', 'tensor'), may hold values from -6 to 6
- key_proj: bfloat16 [8192, 8192], P('context', 'tensor'), may hold values from -6 to 6
- value_proj: bfloat16 [8192, 8192], P('context', 'tensor'), may hold values from -6 to 6
- short_filter: float32 [3, 7, 8192], P(None, None, 'tensor'), may hold values from -2 to 2
- residues: float32 [16, 8192], P(None, 'tensor'), may hold values from -1.5 to 1.5
- decay: float32 [16, 8192], P(None, 'tensor'), may hold values from 0.00012207031 to 0.033333335
- skip_gain: float32 [8192], P('tensor'), may hold values from -6 to 6
- residual: bfloat16 [8192, 8192], P('context', 'tensor'), may hold values from -50 to 50
- norm_gain: float32 [8192], P('tensor'), may hold values from 0.5 to 1.5
Outputs:
- mixed: bfloat16 [8192, 8192], P('context', 'tensor')
- normed: bfloat16 [8192, 8192], P('context', 'tensor')
The draws below stay inside these ranges and needn't reach their ends.
All inputs are finite; a program needn't handle non-finite values.
Results may differ from the reference program's by a relative error of at most 0.014.
Values may be sent and summed in bfloat16 or wider, within the bound.
No kernel may reach another device: no remote copies, remote signals or barrier semaphores. Data moves between devices by JAX's collectives and lax.ppermute only.
A program may use at most 64 MiB of HBM per device.

```python
import math
import jax
import jax.numpy as jnp
from jax import lax

D = 8192
ORDER = 16
SHORT = 7
SEQ = 8192


def draw_residual(key, part):
    row_key, value_key = jax.random.split(key, 2)
    columns = jnp.arange(D).astype(jnp.float32) / D
    row_levels = jax.random.uniform(row_key, (SEQ, 1), jnp.float32)
    factor = jnp.exp(0.5 * math.log(10.0) * (columns[None, :] + row_levels))
    values = jax.random.truncated_normal(value_key, -5.0, 5.0, (SEQ, D), jnp.float32)
    return (values * factor).astype(jnp.bfloat16)


def levels(own_key, dims, shards, smallest, top_value):
    def one(dim, blocks):
        steps = jax.random.uniform(jax.random.fold_in(jax.random.fold_in(own_key, 6), dim), (blocks,), jnp.float32, smallest / len(shards), top_value / len(shards))
        return jnp.repeat(jnp.exp(steps), dims[dim] // blocks).reshape((-1,) + (1,) * (len(dims) - dim - 1))

    factor_of = one(*shards[0])
    for cut in shards[1:]:
        factor_of = factor_of * one(*cut)
    return factor_of


def bell_draw(rng, dims, deviation, limit, cuts=(), kind=jnp.bfloat16):
    values = deviation * jax.random.normal(rng, dims, jnp.float32)
    if cuts:
        values = values * levels(rng, dims, cuts, -0.22, 0.18)
    return jnp.clip(values, -limit, limit).astype(kind)


def setup_inputs(seed: int = 0) -> dict:
    key_list = jax.random.split(jax.random.key(seed), 10)
    query_proj = bell_draw(key_list[0], (SEQ, D), 1.0, 6.0, ((0, 64), (1, 8)))
    key_proj = bell_draw(key_list[1], (SEQ, D), 1.0, 6.0, ((0, 64), (1, 8)))
    value_proj = bell_draw(key_list[2], (SEQ, D), 1.0, 6.0, ((0, 64), (1, 8)))
    short_filter = bell_draw(key_list[3], (3, SHORT, D), SHORT ** -0.5, 2.0, ((2, 8),), jnp.float32)
    residues = bell_draw(key_list[4], (ORDER, D), 0.25, 1.5, ((1, 8),), jnp.float32)
    decay = jnp.clip(jnp.exp(math.log(0.033333335) - 5.609716 * jax.random.uniform(key_list[5], (ORDER, D), jnp.float32) ** levels(key_list[5], (ORDER, D), ((1, 8),), -0.2, 0.2)), 0.00012207031, 0.033333335)
    skip_gain = bell_draw(key_list[6], (D,), 1.0, 6.0, ((0, 8),), jnp.float32)
    residual = draw_residual(jax.random.fold_in(key_list[9], 71), 0)
    norm_gain = jnp.clip(1.0 + 0.1 * jax.random.normal(key_list[8], (D,), jnp.float32), 0.5, 1.5)
    return {"query_proj": query_proj, "key_proj": key_proj, "value_proj": value_proj, "short_filter": short_filter, "residues": residues, "decay": decay, "skip_gain": skip_gain, "residual": residual, "norm_gain": norm_gain}


def short_conv(signal, taps_table):
    tap_count = taps_table.shape[0]
    padded = jnp.pad(signal, ((tap_count - 1, 0), (0, 0)))
    result = padded[tap_count - 1:] * taps_table[0]
    for offset in range(1, tap_count):
        result = result + padded[tap_count - 1 - offset:tap_count - 1 - offset + SEQ] * taps_table[offset]
    return result

def channel_block(pieces):
    query_b, key_b, value_b, filter_b, residue_b, rate_b, skip_b = pieces
    query_conv = short_conv(query_b.astype(jnp.float32), filter_b[0])
    key_conv = short_conv(key_b.astype(jnp.float32), filter_b[1])
    value_conv = short_conv(value_b.astype(jnp.float32), filter_b[2])
    product = key_conv * value_conv
    positions = jnp.arange(SEQ).astype(product.dtype)[:, None]

    def add_mode(index, kernel):
        mode_rate = rate_b[index]
        weight = residue_b[index] * jnp.sqrt(-jnp.expm1(-2.0 * mode_rate))
        return kernel + weight * jnp.exp(-mode_rate * positions)
    kernel = lax.fori_loop(0, ORDER, add_mode, jnp.zeros_like(product))
    spectrum = jnp.fft.rfft(product, n=2 * SEQ, axis=0) * jnp.fft.rfft(kernel, n=2 * SEQ, axis=0)
    long_conv = jnp.fft.irfft(spectrum, n=2 * SEQ, axis=0)[:SEQ].astype(product.dtype)
    gated = query_conv * (long_conv + skip_b * product)
    return gated.astype(jnp.bfloat16)

def reference(query_proj, key_proj, value_proj, short_filter, residues, decay, skip_gain, residual, norm_gain):
    block_width = min(D, 512)
    blocks = D // block_width

    def split_rows(array):
        return array.reshape(SEQ, blocks, block_width).transpose(1, 0, 2)
    filters = short_filter.reshape(3, SHORT, blocks, block_width).transpose(2, 0, 1, 3)
    residue_blocks = residues.reshape(ORDER, blocks, block_width).transpose(1, 0, 2)
    rate_blocks = decay.reshape(ORDER, blocks, block_width).transpose(1, 0, 2)
    skip_blocks = skip_gain.reshape(blocks, block_width)
    outputs = lax.map(channel_block, (split_rows(query_proj), split_rows(key_proj), split_rows(value_proj), filters, residue_blocks, rate_blocks, skip_blocks))
    mixed = outputs.transpose(1, 0, 2).reshape(SEQ, D)
    summed = residual.astype(jnp.float32) + lax.optimization_barrier(mixed).astype(jnp.float32)
    squares = lax.optimization_barrier(jnp.sum(summed * summed, axis=1, keepdims=True))
    normed = (summed * lax.rsqrt(squares / D + 1e-05) * norm_gain).astype(jnp.bfloat16)
    return (mixed, normed)
```

```python
import jax
import jax.numpy as jnp
from jax import lax
from jax.experimental import pallas as pl
from jax.experimental.pallas import tpu as pltpu
from jax.sharding import Mesh, PartitionSpec as P

D = 8192
ORDER = 16
TAPS = 7
ROWS = 128
LANES = 128
GROUPS = 8
BLOCK = 8

f32 = jnp.float32
bf16 = jnp.bfloat16


def stack_rows(dst, src, first, rows, at, step=16):
    for r in range(0, rows, step):
        for j in range(GROUPS):
            tile = src[first + r : first + r + step, j * LANES : (j + 1) * LANES]
            dst[pl.ds((at + r) * GROUPS + j, step, stride=GROUPS), :] = tile.astype(f32)


def stack_taps(dst, taps, which):
    for j in range(GROUPS):
        dst[pl.ds(j, TAPS, stride=GROUPS), :] = taps[which, :, j * LANES : (j + 1) * LANES]


def row(ref, n):
    return ref[pl.ds(pl.multiple_of(n * GROUPS, GROUPS), GROUPS), :]


def put(ref, n, value):
    ref[pl.ds(pl.multiple_of(n * GROUPS, GROUPS), GROUPS), :] = value


def conv(ref, taps, n0, count):
    rows = [row(ref, n0 + 8 - (TAPS - 1) + i) for i in range(count + TAPS - 1)]
    out = []
    for i in range(count):
        total = rows[i + TAPS - 1] * taps[0]
        for j in range(1, TAPS):
            total = total + rows[i + TAPS - 1 - j] * taps[j]
        out.append(total)
    return out


def rows_of(ref, count):
    return [row(ref, m) for m in range(count)]


def total_of(values):
    values = list(values)
    while len(values) > 1:
        values = [a + b for a, b in zip(values[::2], values[1::2])] + (
            [values[-1]] if len(values) % 2 else []
        )
    return values[0]


def call(body, name, outs, scratch, count, scalars=0):
    spec = pl.BlockSpec(memory_space=pltpu.VMEM)
    small = pl.BlockSpec(memory_space=pltpu.SMEM)
    return pl.pallas_call(
        body,
        name=name,
        out_shape=tuple(jax.ShapeDtypeStruct(s, t) for s, t in outs),
        in_specs=[small] * scalars + [spec] * (count - scalars),
        out_specs=tuple(spec for _ in outs),
        scratch_shapes=scratch,
        compiler_params=pltpu.CompilerParams(vmem_limit_bytes=32 << 20),
    )


def local_state(k_ref, v_ref, f_ref, d_ref, u_ref, state_ref, kt, vt, kf, vf, dt):
    stack_taps(kf, f_ref, 1)
    stack_taps(vf, f_ref, 2)
    stack_rows(dt, d_ref, 0, ORDER, 0)
    stack_rows(kt, k_ref, 0, ROWS, 8)
    stack_rows(vt, v_ref, 0, ROWS, 8)
    ktaps, vtaps = rows_of(kf, TAPS), rows_of(vf, TAPS)
    pole = [jnp.exp(-d) for d in rows_of(dt, ORDER)]

    def products(n0, count):
        us = [a * b for a, b in zip(conv(kt, ktaps, n0, count), conv(vt, vtaps, n0, count))]
        for i, u in enumerate(us):
            put(u_ref, n0 + i, u)
        return us

    def advance(state, us):
        for u in us:
            state = [p * s + u for p, s in zip(pole, state)]
        return state

    skip = TAPS - 1
    us = products(skip, BLOCK - skip)
    state = advance([us[0]] * ORDER, us[1:])

    def step(b, state):
        return tuple(advance(list(state), products(b * BLOCK, BLOCK)))

    state = lax.fori_loop(1, ROWS // BLOCK, step, tuple(state))
    for m in range(ORDER):
        put(state_ref, m, state[m])


def edge_state(halo_ref, k_ref, v_ref, f_ref, d_ref, state_ref, out_ref, u_ref, kt, vt, kf, vf, dt):
    stack_taps(kf, f_ref, 1)
    stack_taps(vf, f_ref, 2)
    stack_rows(dt, d_ref, 0, ORDER, 0)
    stack_rows(kt, halo_ref, 8, 8, 0, 8)
    stack_rows(vt, halo_ref, 16, 8, 0, 8)
    stack_rows(kt, k_ref, 0, 8, 8, 8)
    stack_rows(vt, v_ref, 0, 8, 8, 8)
    count = TAPS - 1
    ks = conv(kt, rows_of(kf, TAPS), 0, count)
    vs = conv(vt, rows_of(vf, TAPS), 0, count)
    us = [a * b for a, b in zip(ks, vs)]
    for i, u in enumerate(us):
        put(u_ref, i, u)
    for m in range(0, ORDER, 2):
        pair = []
        for i in (m, m + 1):
            d = row(dt, i)
            p = jnp.exp(-d)
            s = us[0]
            for u in us[1:]:
                s = p * s + u
            pair.append(row(state_ref, i) + jnp.exp(-(ROWS - count) * d) * s)
        both = jnp.concatenate(pair, axis=0).astype(bf16)
        for copy in range(8):
            out_ref[(copy * ORDER + m) * GROUPS : (copy * ORDER + m + 2) * GROUPS, :] = both


def own_part(
    halo_ref, q_ref, u_ref, edge_ref, f_ref, d_ref, w_ref, skip_ref, qc_ref, g_ref, qt, qf, dt, wt, st
):
    stack_taps(qf, f_ref, 0)
    stack_rows(dt, d_ref, 0, ORDER, 0)
    stack_rows(wt, w_ref, 0, ORDER, 0)
    for j in range(GROUPS):
        st[j : j + 1, :] = skip_ref[0:1, j * LANES : (j + 1) * LANES]
    stack_rows(qt, halo_ref, 0, 8, 0, 8)
    stack_rows(qt, q_ref, 0, ROWS, 8)
    taps = rows_of(qf, TAPS)
    pole = [jnp.exp(-d) for d in rows_of(dt, ORDER)]
    weight = rows_of(wt, ORDER)
    gain = st[...]

    def advance(n0, state, us):
        for i, u in enumerate(us):
            state = [p * s + u for p, s in zip(pole, state)]
            put(g_ref, n0 + i, total_of([w * s for w, s in zip(weight, state)] + [gain * u]))
        return state

    def queries(n0):
        for i, c in enumerate(conv(qt, taps, n0, BLOCK)):
            put(qc_ref, n0 + i, c)

    edge = TAPS - 1
    us = rows_of(edge_ref, edge) + [row(u_ref, n) for n in range(edge, BLOCK)]
    zero = jnp.zeros((GROUPS, LANES), f32)
    state = advance(0, [zero] * ORDER, us)
    queries(0)

    def step(b, state):
        n0 = b * BLOCK
        queries(n0)
        return tuple(advance(n0, list(state), [row(u_ref, n0 + i) for i in range(BLOCK)]))

    lax.fori_loop(1, ROWS // BLOCK, step, tuple(state))


def load_pair(ref, block, m):
    both = ref[(block * ORDER + m) * GROUPS : (block * ORDER + m + 2) * GROUPS, :].astype(f32)
    return both[:GROUPS], both[GROUPS:]


def scan_blocks(ref, m, steps, index):
    zero = jnp.zeros((GROUPS, LANES), f32)
    total, before = [zero, zero], [zero, zero]
    for b in range(8):
        here = index == b
        before = [jnp.where(here, t, o) for t, o in zip(total, before)]
        total = [s * t + x for s, t, x in zip(steps, total, load_pair(ref, b, m))]
    return before, total


def scan_near(at_ref, got_ref, d_ref, out_ref, before_ref, dt):
    stack_rows(dt, d_ref, 0, ORDER, 0)
    index = at_ref[1]
    for m in range(0, ORDER, 2):
        steps = [jnp.exp(-float(ROWS) * row(dt, i)) for i in (m, m + 1)]
        before, total = scan_blocks(got_ref, m, steps, index)
        for i in range(2):
            put(before_ref, m + i, before[i])
        both = jnp.concatenate(total, axis=0).astype(bf16)
        for copy in range(8):
            out_ref[(copy * ORDER + m) * GROUPS : (copy * ORDER + m + 2) * GROUPS, :] = both


def finish(
    at_ref, got_ref, before_ref, d_ref, w_ref, qc_ref, g_ref, residual_ref, gain_ref,
    mixed_ref, scaled_ref, squares_ref, dt, wt, st, mt, sq,
):
    stack_rows(dt, d_ref, 0, ORDER, 0)
    stack_rows(wt, w_ref, 0, ORDER, 0)
    far, near = at_ref[0], at_ref[1].astype(f32)
    for m in range(0, ORDER, 2):
        rates = [row(dt, i) for i in (m, m + 1)]
        steps = [jnp.exp(-float(8 * ROWS) * d) for d in rates]
        before, _ = scan_blocks(got_ref, m, steps, far)
        for i in range(2):
            entry = row(before_ref, m + i) + jnp.exp(-float(ROWS) * near * rates[i]) * before[i]
            put(st, m + i, row(wt, m + i) * entry)
    pole = [jnp.exp(-d) for d in rows_of(dt, ORDER)]
    count = 16

    def step(b, state):
        n0 = b * count
        state = list(state)
        for i in range(count):
            state = [p * s for p, s in zip(pole, state)]
            value = row(qc_ref, n0 + i) * (row(g_ref, n0 + i) + total_of(state))
            mt[i * GROUPS : (i + 1) * GROUPS, :] = value
        at = pl.ds(pl.multiple_of(n0, count), count)
        squares = None
        for j in range(GROUPS):
            lanes = slice(j * LANES, (j + 1) * LANES)
            tile = mt[pl.ds(j, count, stride=GROUPS), :].astype(bf16)
            mixed_ref[at, lanes] = tile
            summed = residual_ref[at, lanes].astype(f32) + tile.astype(f32)
            scaled_ref[at, lanes] = summed * gain_ref[0:1, lanes]
            part = summed * summed
            squares = part if squares is None else squares + part
        sq[at, :] = squares
        return tuple(state)

    lax.fori_loop(0, ROWS // count, step, tuple(rows_of(st, ORDER)))
    squares_ref[...] = lax.dot_general(
        jnp.ones((8, LANES), f32), sq[...], (((1,), (1,)), ((), ())),
        precision=lax.Precision.HIGHEST, preferred_element_type=f32,
    )


def normalise(scaled_ref, squares_ref, out_ref):
    total = lax.dot_general(
        squares_ref[...], jnp.ones((8, LANES), f32), (((0,), (0,)), ((), ())),
        precision=lax.Precision.HIGHEST, preferred_element_type=f32,
    )
    factor = lax.rsqrt(total / D + 1e-05)
    for j in range(GROUPS):
        lanes = slice(j * LANES, (j + 1) * LANES)
        out_ref[:, lanes] = (scaled_ref[:, lanes] * factor).astype(bf16)


def shards(query, key, value, short_filter, residues, decay, skip_gain, residual, norm_gain):
    stacked = ((ROWS + 8) * GROUPS, LANES)
    modes = (ORDER * GROUPS, LANES)
    taps = (8 * GROUPS, LANES)
    blocks = (8 * ORDER * GROUPS, LANES)
    whole = (ROWS * GROUPS, LANES)
    vmem = pltpu.VMEM

    weight = residues * jnp.sqrt(-jnp.expm1(-2.0 * decay))
    at = jnp.stack([lax.axis_index("z"), lax.axis_index("y")]).astype(jnp.int32)
    tails = jnp.concatenate([x[ROWS - 8 :] for x in (query, key, value)], axis=0)
    halo = lax.ppermute(tails, ("z", "y"), [(i, i + 1) for i in range(63)])

    u, clean = call(
        local_state, "local_state", [(whole, f32), (modes, f32)],
        [vmem(stacked, f32)] * 2 + [vmem(taps, f32)] * 2 + [vmem(modes, f32)],
        4,
    )(key, value, short_filter, decay)
    sent, edge = call(
        edge_state, "edge_state", [(blocks, bf16), (taps, f32)],
        [vmem((16 * GROUPS, LANES), f32)] * 2 + [vmem(taps, f32)] * 2 + [vmem(modes, f32)],
        6,
    )(halo, key[:16], value[:16], short_filter, decay, clean)
    near = lax.all_to_all(sent, "y", 0, 0, tiled=True)
    qc, own = call(
        own_part, "own_part", [(whole, f32)] * 2,
        [vmem(stacked, f32), vmem(taps, f32)] + [vmem(modes, f32)] * 2 + [vmem((GROUPS, LANES), f32)],
        8,
    )(halo, query, u, edge, short_filter, decay, weight, skip_gain[None])
    totals, before = call(
        scan_near, "scan_near", [(blocks, bf16), (modes, f32)], [vmem(modes, f32)], 3, 1,
    )(at, near, decay)
    far = lax.all_to_all(totals, "z", 0, 0, tiled=True)
    mixed, scaled, squares = call(
        finish, "finish",
        [((ROWS, 1024), bf16), ((ROWS, 1024), f32), ((8, LANES), f32)],
        [vmem(modes, f32)] * 3 + [vmem((16 * GROUPS, LANES), f32), vmem((ROWS, LANES), f32)],
        9, 1,
    )(at, far, before, decay, weight, qc, own, residual, norm_gain[None])
    gathered = lax.all_to_all(squares, "tensor", 0, 0, tiled=True)
    (normed,) = call(normalise, "normalise", [((ROWS, 1024), bf16)], [], 2)(scaled, gathered)
    return mixed, normed


def solution(mesh):
    context = ("z", "y")
    split = Mesh(mesh.devices.reshape(8, 8, 8), ("z", "y", "tensor"))
    rows = P(context, "tensor")
    in_specs = (
        rows, rows, rows, P(None, None, "tensor"), P(None, "tensor"), P(None, "tensor"),
        P("tensor"), rows, P("tensor"),
    )
    return jax.shard_map(shards, mesh=split, in_specs=in_specs, out_specs=(rows, rows), check_vma=False)
```

```python
import jax
import jax.numpy as jnp
from jax import lax
from jax.experimental import pallas as pl
from jax.experimental.pallas import tpu as pltpu
from jax.sharding import Mesh, PartitionSpec as P

D = 8192
ORDER = 16
TAPS = 7
ROWS = 128
LANES = 128
GROUPS = 8
LIMIT = 54300 << 10
BLOCK = 8

f32 = jnp.float32
bf16 = jnp.bfloat16


def stack_rows(dst, src, first, rows, at, step=16):
    for r in range(0, rows, step):
        for j in range(GROUPS):
            tile = src[first + r : first + r + step, j * LANES : (j + 1) * LANES]
            dst[pl.ds((at + r) * GROUPS + j, step, stride=GROUPS), :] = tile.astype(f32)


def stack_taps(dst, taps, which):
    for j in range(GROUPS):
        dst[pl.ds(j, TAPS, stride=GROUPS), :] = taps[which, :, j * LANES : (j + 1) * LANES]


def row(ref, n):
    return ref[pl.ds(pl.multiple_of(n * GROUPS, GROUPS), GROUPS), :]


def put(ref, n, value):
    ref[pl.ds(pl.multiple_of(n * GROUPS, GROUPS), GROUPS), :] = value


def conv(ref, taps, n0, count):
    rows = [row(ref, n0 + 8 - (TAPS - 1) + i) for i in range(count + TAPS - 1)]
    out = []
    for i in range(count):
        total = rows[i + TAPS - 1] * taps[0]
        for j in range(1, TAPS):
            total = total + rows[i + TAPS - 1 - j] * taps[j]
        out.append(total)
    return out


def rows_of(ref, count):
    return [row(ref, m) for m in range(count)]


def total_of(values):
    values = list(values)
    while len(values) > 1:
        values = [a + b for a, b in zip(values[::2], values[1::2])] + (
            [values[-1]] if len(values) % 2 else []
        )
    return values[0]


def call(body, name, outs, scratch, count, scalars=0, far=(), limit=32 << 20, far_out=False):
    spec = pl.BlockSpec(memory_space=pltpu.VMEM)
    kinds = {i: pl.BlockSpec(memory_space=pltpu.SMEM) for i in range(scalars)}
    kinds.update({i: pl.BlockSpec(memory_space=pltpu.HBM) for i in far})
    return pl.pallas_call(
        body,
        name=name,
        out_shape=tuple(jax.ShapeDtypeStruct(s, t) for s, t in outs),
        in_specs=[kinds.get(i, spec) for i in range(count)],
        out_specs=tuple(pl.BlockSpec(memory_space=pltpu.HBM) if far_out else spec for _ in outs),
        scratch_shapes=scratch,
        compiler_params=pltpu.CompilerParams(vmem_limit_bytes=limit),
    )


def fetch(q_hbm, k_hbm, v_hbm, tails, q_out, k_out, v_out, sems):
    copies = []
    for i, (src, dst) in enumerate(((q_hbm, q_out), (k_hbm, k_out), (v_hbm, v_out))):
        ends = src.at[pl.ds(ROWS - 8, 8)], tails.at[pl.ds(8 * i, 8)]
        copies.append(pltpu.make_async_copy(*ends, sems.at[0, i]))
        copies.append(pltpu.make_async_copy(src, dst, sems.at[1, i]))
    for copy in copies[::2] + copies[1::2]:
        copy.start()
    for copy in copies:
        copy.wait()


def one_less_exp(d):
    square = d * d
    series = 1.0 + square / 72.0
    for divisor in (42.0, 20.0, 6.0):
        series = 1.0 + square * (1.0 / divisor) * series
    return 2.0 * jnp.exp(-d) * d * series


def local_part(
    at_ref, q_ref, k_ref, v_ref, f_ref, d_ref, r_ref, skip_ref, gain_ref,
    qc_ref, g_ref, state_ref, taps_ref, heads_ref, dt, wt, st, gain_out, qt, kt, vt, rt,
):
    del at_ref
    gain_out[...] = gain_ref[...]
    for i, (src, dst) in enumerate(((q_ref, qt), (k_ref, kt), (v_ref, vt))):
        stack_taps(taps_ref.at[pl.ds(8 * GROUPS * i, 8 * GROUPS)], f_ref, i)
        stack_rows(dst, src, 0, ROWS, 8)
        heads_ref[8 * GROUPS * i : 8 * GROUPS * (i + 1), :] = dst[8 * GROUPS : 16 * GROUPS, :]
    stack_rows(dt, d_ref, 0, ORDER, 0)
    stack_rows(rt, r_ref, 0, ORDER, 0)
    wt[...] = rt[...] * jnp.sqrt(one_less_exp(dt[...]))
    for j in range(GROUPS):
        st[j : j + 1, :] = skip_ref[0:1, j * LANES : (j + 1) * LANES]
    taps = [[row(taps_ref, 8 * i + j) for j in range(TAPS)] for i in range(3)]
    pole = [jnp.exp(-d) for d in rows_of(dt, ORDER)]
    skip = st[...]

    def block(n0, count, state):
        for i, c in enumerate(conv(qt, taps[0], n0, count)):
            put(qc_ref, n0 + i, c)
        us = [a * b for a, b in zip(conv(kt, taps[1], n0, count), conv(vt, taps[2], n0, count))]
        for i, u in enumerate(us):
            state = [u] * ORDER if state is None else [p * s + u for p, s in zip(pole, state)]
            terms = [row(wt, m) * s for m, s in enumerate(state)]
            put(g_ref, n0 + i, total_of(terms + [skip * u]))
        return state

    edge = TAPS - 1
    state = block(edge, BLOCK - edge, None)
    state = lax.fori_loop(
        1, ROWS // BLOCK, lambda b, s: tuple(block(b * BLOCK, BLOCK, list(s))), tuple(state)
    )
    for m in range(ORDER):
        put(state_ref, m, state[m])


def edge_part(halo_ref, heads_ref, taps_ref, dt, state_ref, out_ref, edge_ref, xt):
    edge = TAPS - 1
    convs = []
    for i in range(3):
        at = xt.at[pl.ds(16 * GROUPS * i, 16 * GROUPS)]
        stack_rows(at, halo_ref, 8 * i, 8, 0, 8)
        at[8 * GROUPS : 16 * GROUPS, :] = heads_ref[8 * GROUPS * i : 8 * GROUPS * (i + 1), :]
        convs.append(conv(at, [row(taps_ref, 8 * i + j) for j in range(TAPS)], 0, edge))
    us = [a * b for a, b in zip(convs[1], convs[2])]
    for i in range(edge):
        put(edge_ref, i, us[i])
        put(edge_ref, 8 + i, convs[0][i])
    for m in range(0, ORDER, 2):
        pair = []
        for i in (m, m + 1):
            d = row(dt, i)
            p = jnp.exp(-d)
            s = us[0]
            for u in us[1:]:
                s = p * s + u
            pair.append(row(state_ref, i) + jnp.exp(-(ROWS - edge) * d) * s)
        both = jnp.concatenate(pair, axis=0).astype(bf16)
        for copy in range(8):
            out_ref[(copy * ORDER + m) * GROUPS : (copy * ORDER + m + 2) * GROUPS, :] = both


def load_pair(ref, block, m):
    both = ref[(block * ORDER + m) * GROUPS : (block * ORDER + m + 2) * GROUPS, :].astype(f32)
    return both[:GROUPS], both[GROUPS:]


def scan_blocks(ref, m, steps, index):
    zero = jnp.zeros((GROUPS, LANES), f32)
    total, before = [zero, zero], [zero, zero]
    for b in range(8):
        here = index == b
        before = [jnp.where(here, t, o) for t, o in zip(total, before)]
        total = [s * t + x for s, t, x in zip(steps, total, load_pair(ref, b, m))]
    return before, total


def scan_near(at_ref, got_ref, dt, out_ref, before_ref):
    index = at_ref[1]
    for m in range(0, ORDER, 2):
        steps = [jnp.exp(-float(ROWS) * row(dt, i)) for i in (m, m + 1)]
        before, total = scan_blocks(got_ref, m, steps, index)
        for i in range(2):
            put(before_ref, m + i, before[i])
        both = jnp.concatenate(total, axis=0).astype(bf16)
        for copy in range(8):
            out_ref[(copy * ORDER + m) * GROUPS : (copy * ORDER + m + 2) * GROUPS, :] = both


def finish(
    at_ref, got_ref, before_ref, dt, wt, skip_ref, qc_ref, g_ref, edge_ref, residual_ref, gain_ref,
    mixed_ref, scaled_ref, squares_ref, st, mt, sq,
):
    far, near = at_ref[0], at_ref[1].astype(f32)
    for m in range(0, ORDER, 2):
        rates = [row(dt, i) for i in (m, m + 1)]
        steps = [jnp.exp(-float(8 * ROWS) * d) for d in rates]
        before, _ = scan_blocks(got_ref, m, steps, far)
        for i in range(2):
            entry = row(before_ref, m + i) + jnp.exp(-float(ROWS) * near * rates[i]) * before[i]
            put(st, m + i, row(wt, m + i) * entry)
    pole = [jnp.exp(-d) for d in rows_of(dt, ORDER)]
    skip = skip_ref[...]
    count = 16

    def block(n0, state, edge):
        state = list(state)
        for i in range(count):
            state = [p * s for p, s in zip(pole, state)]
            if i < edge:
                u = row(edge_ref, i)
                state = [s + row(wt, m) * u for m, s in enumerate(state)]
                value = row(edge_ref, 8 + i) * (skip * u + total_of(state))
            else:
                value = row(qc_ref, n0 + i) * (row(g_ref, n0 + i) + total_of(state))
            mt[i * GROUPS : (i + 1) * GROUPS, :] = value
        at = pl.ds(pl.multiple_of(n0, count), count)
        squares = None
        for j in range(GROUPS):
            lanes = slice(j * LANES, (j + 1) * LANES)
            tile = mt[pl.ds(j, count, stride=GROUPS), :].astype(bf16)
            mixed_ref[at, lanes] = tile
            summed = residual_ref[at, lanes].astype(f32) + tile.astype(f32)
            scaled_ref[at, lanes] = summed * gain_ref[0:1, lanes]
            part = summed * summed
            squares = part if squares is None else squares + part
        sq[at, :] = squares
        return tuple(state)

    state = block(0, rows_of(st, ORDER), TAPS - 1)
    lax.fori_loop(1, ROWS // count, lambda b, s: block(b * count, s, 0), state)
    squares_ref[...] = lax.dot_general(
        jnp.ones((8, LANES), f32), sq[...], (((1,), (1,)), ((), ())),
        precision=lax.Precision.HIGHEST, preferred_element_type=f32,
    )


def normalise(mixed_ref, scaled_ref, squares_ref, mixed_hbm, out_hbm, out, sems):
    first = pltpu.make_async_copy(mixed_ref, mixed_hbm, sems.at[0])
    first.start()
    total = lax.dot_general(
        squares_ref[...], jnp.ones((8, LANES), f32), (((0,), (0,)), ((), ())),
        precision=lax.Precision.HIGHEST, preferred_element_type=f32,
    )
    factor = lax.rsqrt(total / D + 1e-05)
    half = ROWS // 2
    copies = [first]
    for part in range(2):
        rows = slice(part * half, (part + 1) * half)
        for j in range(GROUPS):
            lanes = slice(j * LANES, (j + 1) * LANES)
            out[rows, lanes] = (scaled_ref[rows, lanes] * factor[rows]).astype(bf16)
        at = pl.ds(part * half, half)
        copy = pltpu.make_async_copy(out.at[at], out_hbm.at[at], sems.at[1 + part])
        copy.start()
        copies.append(copy)
    for copy in copies:
        copy.wait()


def shards(query, key, value, short_filter, residues, decay, skip_gain, residual, norm_gain):
    stacked = ((ROWS + 8) * GROUPS, LANES)
    modes = (ORDER * GROUPS, LANES)
    taps = (24 * GROUPS, LANES)
    blocks = (8 * ORDER * GROUPS, LANES)
    whole = (ROWS * GROUPS, LANES)
    natural = (ROWS, query.shape[1])
    vmem = pltpu.VMEM

    at = jnp.stack([lax.axis_index("z"), lax.axis_index("y")]).astype(jnp.int32)
    tails, q_here, k_here, v_here = call(
        fetch, "fetch", [((24, natural[1]), bf16)] + [(natural, bf16)] * 3, [pltpu.SemaphoreType.DMA((2, 3))],
        3, far=(0, 1, 2), limit=LIMIT,
    )(query, key, value)
    halo = lax.ppermute(tails, ("z", "y"), [(i, i + 1) for i in range(63)])
    qc, own, clean, taps_t, heads, rates, weights, skip, gain = call(
        local_part, "local_part",
        [(whole, f32)] * 2 + [(modes, f32)] + [(taps, f32)] * 2 + [(modes, f32)] * 2
        + [((GROUPS, LANES), f32), ((1, natural[1]), f32)],
        [vmem(stacked, f32)] * 3 + [vmem(modes, f32)], 9, 1,
    )(at, q_here, k_here, v_here, short_filter, decay, residues, skip_gain[None], norm_gain[None])
    sent, edge = call(
        edge_part, "edge_part", [(blocks, bf16), ((16 * GROUPS, LANES), f32)], [vmem((48 * GROUPS, LANES), f32)], 5,
    )(halo, heads, taps_t, rates, clean)
    near = lax.all_to_all(sent, "y", 0, 0, tiled=True)
    totals, before = call(
        scan_near, "scan_near", [(blocks, bf16), (modes, f32)], [], 3, 1,
    )(at, near, rates)
    far = lax.all_to_all(totals, "z", 0, 0, tiled=True)
    mixed, scaled, squares = call(
        finish, "finish",
        [(natural, bf16), (natural, f32), ((8, LANES), f32)],
        [vmem(modes, f32), vmem((16 * GROUPS, LANES), f32), vmem((ROWS, LANES), f32)],
        11, 1,
    )(at, far, before, rates, weights, skip, qc, own, edge, residual, gain)
    gathered = lax.all_to_all(squares, "tensor", 0, 0, tiled=True)
    return call(
        normalise, "normalise", [(natural, bf16)] * 2, [vmem(natural, bf16), pltpu.SemaphoreType.DMA((3,))],
        3, far_out=True,
    )(mixed, scaled, gathered)


def solution(mesh):
    context = ("z", "y")
    split = Mesh(mesh.devices.reshape(8, 8, 8), ("z", "y", "tensor"))
    rows = P(context, "tensor")
    in_specs = (
        rows, rows, rows, P(None, None, "tensor"), P(None, "tensor"), P(None, "tensor"),
        P("tensor"), rows, P("tensor"),
    )
    return jax.shard_map(shards, mesh=split, in_specs=in_specs, out_specs=(rows, rows), check_vma=False)
```

```python
import jax
import jax.numpy as jnp
from jax import lax
from jax.experimental import pallas as pl
from jax.experimental.pallas import tpu as pltpu
from jax.sharding import Mesh, PartitionSpec as P

D = 8192
ORDER = 16
TAPS = 7
ROWS = 128
LANES = 128
GROUPS = 8
LIMIT = 54300 << 10
CONTEXT = ("half", "place", "y")
BLOCK = 8

f32 = jnp.float32
bf16 = jnp.bfloat16


def stack_rows(dst, src, first, rows, at, step=16):
    for r in range(0, rows, step):
        for j in range(GROUPS):
            tile = src[first + r : first + r + step, j * LANES : (j + 1) * LANES]
            dst[pl.ds((at + r) * GROUPS + j, step, stride=GROUPS), :] = tile.astype(f32)


def stack_taps(dst, taps, which):
    for j in range(GROUPS):
        dst[pl.ds(j, TAPS, stride=GROUPS), :] = taps[which, :, j * LANES : (j + 1) * LANES]


def row(ref, n):
    return ref[pl.ds(pl.multiple_of(n * GROUPS, GROUPS), GROUPS), :]


def put(ref, n, value):
    ref[pl.ds(pl.multiple_of(n * GROUPS, GROUPS), GROUPS), :] = value


def conv(ref, taps, n0, count):
    rows = [row(ref, n0 + 8 - (TAPS - 1) + i) for i in range(count + TAPS - 1)]
    out = []
    for i in range(count):
        total = rows[i + TAPS - 1] * taps[0]
        for j in range(1, TAPS):
            total = total + rows[i + TAPS - 1 - j] * taps[j]
        out.append(total)
    return out


def rows_of(ref, count):
    return [row(ref, m) for m in range(count)]


def total_of(values):
    values = list(values)
    while len(values) > 1:
        values = [a + b for a, b in zip(values[::2], values[1::2])] + (
            [values[-1]] if len(values) % 2 else []
        )
    return values[0]


def call(body, name, outs, scratch, count, scalars=0, far=(), limit=32 << 20, far_out=False):
    spec = pl.BlockSpec(memory_space=pltpu.VMEM)
    kinds = {i: pl.BlockSpec(memory_space=pltpu.SMEM) for i in range(scalars)}
    kinds.update({i: pl.BlockSpec(memory_space=pltpu.HBM) for i in far})
    return pl.pallas_call(
        body,
        name=name,
        out_shape=tuple(jax.ShapeDtypeStruct(s, t) for s, t in outs),
        in_specs=[kinds.get(i, spec) for i in range(count)],
        out_specs=tuple(pl.BlockSpec(memory_space=pltpu.HBM) if far_out else spec for _ in outs),
        scratch_shapes=scratch,
        compiler_params=pltpu.CompilerParams(vmem_limit_bytes=limit),
    )


def fetch(q_hbm, k_hbm, v_hbm, tails, q_out, k_out, v_out, sems):
    copies = []
    for i, (src, dst) in enumerate(((q_hbm, q_out), (k_hbm, k_out), (v_hbm, v_out))):
        ends = src.at[pl.ds(ROWS - 8, 8)], tails.at[pl.ds(8 * i, 8)]
        copies.append(pltpu.make_async_copy(*ends, sems.at[0, i]))
        copies.append(pltpu.make_async_copy(src, dst, sems.at[1, i]))
    for copy in copies[::2] + copies[1::2]:
        copy.start()
    for copy in copies:
        copy.wait()


def one_less_exp(d):
    square = d * d
    series = 1.0 + square / 72.0
    for divisor in (42.0, 20.0, 6.0):
        series = 1.0 + square * (1.0 / divisor) * series
    return 2.0 * jnp.exp(-d) * d * series


def local_part(
    at_ref, q_ref, k_ref, v_ref, f_ref, d_ref, r_ref, skip_ref, gain_ref,
    qc_ref, g_ref, state_ref, taps_ref, heads_ref, dt, wt, st, gain_out, qt, kt, vt, rt,
):
    del at_ref
    gain_out[...] = gain_ref[...]
    for i, (src, dst) in enumerate(((q_ref, qt), (k_ref, kt), (v_ref, vt))):
        stack_taps(taps_ref.at[pl.ds(8 * GROUPS * i, 8 * GROUPS)], f_ref, i)
        stack_rows(dst, src, 0, ROWS, 8)
        heads_ref[8 * GROUPS * i : 8 * GROUPS * (i + 1), :] = dst[8 * GROUPS : 16 * GROUPS, :]
    stack_rows(dt, d_ref, 0, ORDER, 0)
    stack_rows(rt, r_ref, 0, ORDER, 0)
    wt[...] = rt[...] * jnp.sqrt(one_less_exp(dt[...]))
    for j in range(GROUPS):
        st[j : j + 1, :] = skip_ref[0:1, j * LANES : (j + 1) * LANES]
    taps = [[row(taps_ref, 8 * i + j) for j in range(TAPS)] for i in range(3)]
    pole = [jnp.exp(-d) for d in rows_of(dt, ORDER)]
    skip = st[...]

    def block(n0, count, state):
        for i, c in enumerate(conv(qt, taps[0], n0, count)):
            put(qc_ref, n0 + i, c)
        us = [a * b for a, b in zip(conv(kt, taps[1], n0, count), conv(vt, taps[2], n0, count))]
        for i, u in enumerate(us):
            state = [u] * ORDER if state is None else [p * s + u for p, s in zip(pole, state)]
            terms = [row(wt, m) * s for m, s in enumerate(state)]
            put(g_ref, n0 + i, total_of(terms + [skip * u]))
        return state

    edge = TAPS - 1
    state = block(edge, BLOCK - edge, None)
    state = lax.fori_loop(
        1, ROWS // BLOCK, lambda b, s: tuple(block(b * BLOCK, BLOCK, list(s))), tuple(state)
    )
    for m in range(ORDER):
        put(state_ref, m, state[m])


def edge_part(halo_ref, heads_ref, taps_ref, dt, state_ref, out_ref, edge_ref, xt):
    edge = TAPS - 1
    convs = []
    for i in range(3):
        at = xt.at[pl.ds(16 * GROUPS * i, 16 * GROUPS)]
        stack_rows(at, halo_ref, 8 * i, 8, 0, 8)
        at[8 * GROUPS : 16 * GROUPS, :] = heads_ref[8 * GROUPS * i : 8 * GROUPS * (i + 1), :]
        convs.append(conv(at, [row(taps_ref, 8 * i + j) for j in range(TAPS)], 0, edge))
    us = [a * b for a, b in zip(convs[1], convs[2])]
    for i in range(edge):
        put(edge_ref, i, us[i])
        put(edge_ref, 8 + i, convs[0][i])
    for m in range(0, ORDER, 2):
        pair = []
        for i in (m, m + 1):
            d = row(dt, i)
            p = jnp.exp(-d)
            s = us[0]
            for u in us[1:]:
                s = p * s + u
            pair.append(row(state_ref, i) + jnp.exp(-(ROWS - edge) * d) * s)
        both = jnp.concatenate(pair, axis=0).astype(bf16)
        for copy in range(8):
            out_ref[(copy * ORDER + m) * GROUPS : (copy * ORDER + m + 2) * GROUPS, :] = both


def load_pair(ref, block, m):
    both = ref[(block * ORDER + m) * GROUPS : (block * ORDER + m + 2) * GROUPS, :].astype(f32)
    return both[:GROUPS], both[GROUPS:]


def scan_blocks(ref, m, steps, count, index=None):
    total = load_pair(ref, 0, m)
    before = [jnp.zeros_like(total[0])] * 2
    for b in range(1, count):
        if index is not None:
            before = [jnp.where(index == b, t, o) for t, o in zip(total, before)]
        total = [s * t + x for s, t, x in zip(steps, total, load_pair(ref, b, m))]
    return before, total


def scan_near(at_ref, got_ref, dt, out_ref, before_ref):
    index = at_ref[2]
    for m in range(0, ORDER, 2):
        steps = [jnp.exp(-float(ROWS) * row(dt, i)) for i in (m, m + 1)]
        before, total = scan_blocks(got_ref, m, steps, 8, index)
        for i in range(2):
            put(before_ref, m + i, before[i])
        both = jnp.concatenate(total, axis=0).astype(bf16)
        for copy in range(4):
            out_ref[(copy * ORDER + m) * GROUPS : (copy * ORDER + m + 2) * GROUPS, :] = both


def sum_half(got_ref, dt, out_ref):
    for m in range(0, ORDER, 2):
        steps = [jnp.exp(-float(8 * ROWS) * row(dt, i)) for i in (m, m + 1)]
        _, total = scan_blocks(got_ref, m, steps, 4)
        out_ref[m * GROUPS : (m + 2) * GROUPS, :] = jnp.concatenate(total, axis=0).astype(bf16)


def finish(
    at_ref, got_ref, half_ref, before_ref, dt, wt, skip_ref, qc_ref, g_ref, edge_ref, residual_ref, gain_ref,
    mixed_ref, scaled_ref, squares_ref, st, mt, sq,
):
    place, place_f, near = at_ref[1], at_ref[1].astype(f32), at_ref[2].astype(f32)
    for m in range(0, ORDER, 2):
        rates = [row(dt, i) for i in (m, m + 1)]
        steps = [jnp.exp(-float(8 * ROWS) * d) for d in rates]
        far, _ = scan_blocks(got_ref, m, steps, 4, place)
        halves = load_pair(half_ref, 0, m)
        for i in range(2):
            far_i = far[i] + jnp.exp(-float(8 * ROWS) * place_f * rates[i]) * halves[i]
            entry = row(before_ref, m + i) + jnp.exp(-float(ROWS) * near * rates[i]) * far_i
            put(st, m + i, row(wt, m + i) * entry)
    pole = [jnp.exp(-d) for d in rows_of(dt, ORDER)]
    skip = skip_ref[...]
    count = 16

    def block(n0, state, edge):
        state = list(state)
        for i in range(count):
            state = [p * s for p, s in zip(pole, state)]
            if i < edge:
                u = row(edge_ref, i)
                state = [s + row(wt, m) * u for m, s in enumerate(state)]
                value = row(edge_ref, 8 + i) * (skip * u + total_of(state))
            else:
                value = row(qc_ref, n0 + i) * (row(g_ref, n0 + i) + total_of(state))
            mt[i * GROUPS : (i + 1) * GROUPS, :] = value
        at = pl.ds(pl.multiple_of(n0, count), count)
        squares = None
        for j in range(GROUPS):
            lanes = slice(j * LANES, (j + 1) * LANES)
            tile = mt[pl.ds(j, count, stride=GROUPS), :].astype(bf16)
            mixed_ref[at, lanes] = tile
            summed = residual_ref[at, lanes].astype(f32) + tile.astype(f32)
            scaled_ref[at, lanes] = summed * gain_ref[0:1, lanes]
            part = summed * summed
            squares = part if squares is None else squares + part
        sq[at, :] = squares
        return tuple(state)

    state = block(0, rows_of(st, ORDER), TAPS - 1)
    lax.fori_loop(1, ROWS // count, lambda b, s: block(b * count, s, 0), state)
    squares_ref[...] = lax.dot_general(
        jnp.ones((8, LANES), f32), sq[...], (((1,), (1,)), ((), ())),
        precision=lax.Precision.HIGHEST, preferred_element_type=f32,
    )


def normalise(mixed_ref, scaled_ref, squares_ref, mixed_hbm, out_hbm, out, sems):
    first = pltpu.make_async_copy(mixed_ref, mixed_hbm, sems.at[0])
    first.start()
    total = lax.dot_general(
        squares_ref[...], jnp.ones((8, LANES), f32), (((0,), (0,)), ((), ())),
        precision=lax.Precision.HIGHEST, preferred_element_type=f32,
    )
    factor = lax.rsqrt(total / D + 1e-05)
    half = ROWS // 2
    copies = [first]
    for part in range(2):
        rows = slice(part * half, (part + 1) * half)
        for j in range(GROUPS):
            lanes = slice(j * LANES, (j + 1) * LANES)
            out[rows, lanes] = (scaled_ref[rows, lanes] * factor[rows]).astype(bf16)
        at = pl.ds(part * half, half)
        copy = pltpu.make_async_copy(out.at[at], out_hbm.at[at], sems.at[1 + part])
        copy.start()
        copies.append(copy)
    for copy in copies:
        copy.wait()


def shards(query, key, value, short_filter, residues, decay, skip_gain, residual, norm_gain):
    stacked = ((ROWS + 8) * GROUPS, LANES)
    modes = (ORDER * GROUPS, LANES)
    taps = (24 * GROUPS, LANES)
    blocks = (8 * ORDER * GROUPS, LANES)
    quads = (4 * ORDER * GROUPS, LANES)
    whole = (ROWS * GROUPS, LANES)
    natural = (ROWS, query.shape[1])
    vmem = pltpu.VMEM

    at = jnp.stack([lax.axis_index(name) for name in CONTEXT]).astype(jnp.int32)
    tails, q_here, k_here, v_here = call(
        fetch, "fetch", [((24, natural[1]), bf16)] + [(natural, bf16)] * 3, [pltpu.SemaphoreType.DMA((2, 3))],
        3, far=(0, 1, 2), limit=LIMIT,
    )(query, key, value)
    halo = lax.ppermute(tails, CONTEXT, [(i, i + 1) for i in range(63)])
    qc, own, clean, taps_t, heads, rates, weights, skip, gain = call(
        local_part, "local_part",
        [(whole, f32)] * 2 + [(modes, f32)] + [(taps, f32)] * 2 + [(modes, f32)] * 2
        + [((GROUPS, LANES), f32), ((1, natural[1]), f32)],
        [vmem(stacked, f32)] * 3 + [vmem(modes, f32)], 9, 1,
    )(at, q_here, k_here, v_here, short_filter, decay, residues, skip_gain[None], norm_gain[None])
    sent, edge = call(
        edge_part, "edge_part", [(blocks, bf16), ((16 * GROUPS, LANES), f32)], [vmem((48 * GROUPS, LANES), f32)], 5,
    )(halo, heads, taps_t, rates, clean)
    near = lax.all_to_all(sent, "y", 0, 0, tiled=True)
    totals, before = call(
        scan_near, "scan_near", [(quads, bf16), (modes, f32)], [], 3, 1,
    )(at, near, rates)

    def exchange(x, _):
        return lax.all_to_all(x, "place", 0, 0, tiled=True)

    totals, second = lax.optimization_barrier((totals, at[0]))
    quad = lax.switch(second, (exchange, lambda x, _: x), totals, totals)
    half, = call(sum_half, "sum_half", [(modes, bf16)], [], 2)(quad, rates)
    carried = lax.ppermute(half, "half", [(0, 1)])
    totals, half = lax.optimization_barrier((totals, half))
    quad = lax.switch(second, (lambda _, y: y, exchange), totals, quad)
    mixed, scaled, squares = call(
        finish, "finish",
        [(natural, bf16), (natural, f32), ((8, LANES), f32)],
        [vmem(modes, f32), vmem((16 * GROUPS, LANES), f32), vmem((ROWS, LANES), f32)],
        12, 1,
    )(at, quad, carried, before, rates, weights, skip, qc, own, edge, residual, gain)
    gathered = lax.all_to_all(squares, "tensor", 0, 0, tiled=True)
    return call(
        normalise, "normalise", [(natural, bf16)] * 2, [vmem(natural, bf16), pltpu.SemaphoreType.DMA((3,))],
        3, far_out=True,
    )(mixed, scaled, gathered)


def solution(mesh):
    split = Mesh(mesh.devices.reshape(2, 4, 8, 8), CONTEXT + ("tensor",))
    rows = P(CONTEXT, "tensor")
    in_specs = (
        rows, rows, rows, P(None, None, "tensor"), P(None, "tensor"), P(None, "tensor"),
        P("tensor"), rows, P("tensor"),
    )
    return jax.shard_map(shards, mesh=split, in_specs=in_specs, out_specs=(rows, rows), check_vma=False)
```

```python
import jax
import jax.numpy as jnp
from jax import lax
from jax.experimental import pallas as pl
from jax.experimental.pallas import tpu as pltpu
from jax.sharding import Mesh, PartitionSpec as P

D = 8192
ORDER = 16
TAPS = 7
ROWS = 128
LANES = 128
GROUPS = 8
LIMIT = 54300 << 10
CONTEXT = ("half", "place", "y")
Z = CONTEXT[:2]
BLOCK = 8

f32 = jnp.float32
bf16 = jnp.bfloat16


def stack_rows(dst, src, first, rows, at, step=16):
    for r in range(0, rows, step):
        for j in range(GROUPS):
            tile = src[first + r : first + r + step, j * LANES : (j + 1) * LANES]
            dst[pl.ds((at + r) * GROUPS + j, step, stride=GROUPS), :] = tile.astype(f32)


def stack_taps(dst, taps, which):
    for j in range(GROUPS):
        dst[pl.ds(j, TAPS, stride=GROUPS), :] = taps[which, :, j * LANES : (j + 1) * LANES]


def row(ref, n):
    return ref[pl.ds(pl.multiple_of(n * GROUPS, GROUPS), GROUPS), :]


def put(ref, n, value):
    ref[pl.ds(pl.multiple_of(n * GROUPS, GROUPS), GROUPS), :] = value


def conv(ref, taps, n0, count):
    rows = [row(ref, n0 + 8 - (TAPS - 1) + i) for i in range(count + TAPS - 1)]
    out = []
    for i in range(count):
        total = rows[i + TAPS - 1] * taps[0]
        for j in range(1, TAPS):
            total = total + rows[i + TAPS - 1 - j] * taps[j]
        out.append(total)
    return out


def rows_of(ref, count):
    return [row(ref, m) for m in range(count)]


def total_of(values):
    values = list(values)
    while len(values) > 1:
        values = [a + b for a, b in zip(values[::2], values[1::2])] + (
            [values[-1]] if len(values) % 2 else []
        )
    return values[0]


def call(body, name, outs, scratch, count, scalars=0, far=(), limit=32 << 20, far_out=False):
    spec = pl.BlockSpec(memory_space=pltpu.VMEM)
    kinds = {i: pl.BlockSpec(memory_space=pltpu.SMEM) for i in range(scalars)}
    kinds.update({i: pl.BlockSpec(memory_space=pltpu.HBM) for i in far})
    return pl.pallas_call(
        body,
        name=name,
        out_shape=tuple(jax.ShapeDtypeStruct(s, t) for s, t in outs),
        in_specs=[kinds.get(i, spec) for i in range(count)],
        out_specs=tuple(pl.BlockSpec(memory_space=pltpu.HBM) if far_out else spec for _ in outs),
        scratch_shapes=scratch,
        compiler_params=pltpu.CompilerParams(vmem_limit_bytes=limit),
    )


def fetch(q_hbm, k_hbm, v_hbm, tails, q_out, k_out, v_out, sems):
    copies = []
    for i, (src, dst) in enumerate(((q_hbm, q_out), (k_hbm, k_out), (v_hbm, v_out))):
        ends = src.at[pl.ds(ROWS - 8, 8)], tails.at[pl.ds(8 * i, 8)]
        copies.append(pltpu.make_async_copy(*ends, sems.at[0, i]))
        copies.append(pltpu.make_async_copy(src, dst, sems.at[1, i]))
    for copy in copies[::2] + copies[1::2]:
        copy.start()
    for copy in copies:
        copy.wait()


def one_less_exp(d):
    square = d * d
    series = 1.0 + square / 72.0
    for divisor in (42.0, 20.0, 6.0):
        series = 1.0 + square * (1.0 / divisor) * series
    return 2.0 * jnp.exp(-d) * d * series


def local_part(
    at_ref, q_ref, k_ref, v_ref, f_ref, d_ref, r_ref, skip_ref, gain_ref,
    qc_ref, g_ref, state_ref, taps_ref, heads_ref, dt, wt, st, gain_out, qt, kt, vt, rt,
):
    del at_ref
    gain_out[...] = gain_ref[...]
    for i, (src, dst) in enumerate(((q_ref, qt), (k_ref, kt), (v_ref, vt))):
        stack_taps(taps_ref.at[pl.ds(8 * GROUPS * i, 8 * GROUPS)], f_ref, i)
        stack_rows(dst, src, 0, ROWS, 8)
        heads_ref[8 * GROUPS * i : 8 * GROUPS * (i + 1), :] = dst[8 * GROUPS : 16 * GROUPS, :]
    stack_rows(dt, d_ref, 0, ORDER, 0)
    stack_rows(rt, r_ref, 0, ORDER, 0)
    wt[...] = rt[...] * jnp.sqrt(one_less_exp(dt[...]))
    for j in range(GROUPS):
        st[j : j + 1, :] = skip_ref[0:1, j * LANES : (j + 1) * LANES]
    taps = [[row(taps_ref, 8 * i + j) for j in range(TAPS)] for i in range(3)]
    pole = [jnp.exp(-d) for d in rows_of(dt, ORDER)]
    skip = st[...]

    def block(n0, count, state):
        for i, c in enumerate(conv(qt, taps[0], n0, count)):
            put(qc_ref, n0 + i, c)
        us = [a * b for a, b in zip(conv(kt, taps[1], n0, count), conv(vt, taps[2], n0, count))]
        for i, u in enumerate(us):
            state = [u] * ORDER if state is None else [p * s + u for p, s in zip(pole, state)]
            terms = [row(wt, m) * s for m, s in enumerate(state)]
            put(g_ref, n0 + i, total_of(terms + [skip * u]))
        return state

    edge = TAPS - 1
    state = block(edge, BLOCK - edge, None)
    state = lax.fori_loop(
        1, ROWS // BLOCK, lambda b, s: tuple(block(b * BLOCK, BLOCK, list(s))), tuple(state)
    )
    for m in range(ORDER):
        put(state_ref, m, state[m])


def edge_part(halo_ref, heads_ref, taps_ref, dt, state_ref, out_ref, edge_ref, xt):
    edge = TAPS - 1
    convs = []
    for i in range(3):
        at = xt.at[pl.ds(16 * GROUPS * i, 16 * GROUPS)]
        stack_rows(at, halo_ref, 8 * i, 8, 0, 8)
        at[8 * GROUPS : 16 * GROUPS, :] = heads_ref[8 * GROUPS * i : 8 * GROUPS * (i + 1), :]
        convs.append(conv(at, [row(taps_ref, 8 * i + j) for j in range(TAPS)], 0, edge))
    us = [a * b for a, b in zip(convs[1], convs[2])]
    for i in range(edge):
        put(edge_ref, i, us[i])
        put(edge_ref, 8 + i, convs[0][i])
    for m in range(0, ORDER, 2):
        pair = []
        for i in (m, m + 1):
            d = row(dt, i)
            p = jnp.exp(-d)
            s = us[0]
            for u in us[1:]:
                s = p * s + u
            pair.append(row(state_ref, i) + jnp.exp(-(ROWS - edge) * d) * s)
        both = jnp.concatenate(pair, axis=0).astype(bf16)
        for copy in range(8):
            out_ref[(copy * ORDER + m) * GROUPS : (copy * ORDER + m + 2) * GROUPS, :] = both


def load_pair(ref, block, m):
    both = ref[(block * ORDER + m) * GROUPS : (block * ORDER + m + 2) * GROUPS, :].astype(f32)
    return both[:GROUPS], both[GROUPS:]


def scan_blocks(ref, m, steps, count, index=None):
    total = load_pair(ref, 0, m)
    before = [jnp.zeros_like(total[0])] * 2
    for b in range(1, count):
        if index is not None:
            before = [jnp.where(index == b, t, o) for t, o in zip(total, before)]
        total = [s * t + x for s, t, x in zip(steps, total, load_pair(ref, b, m))]
    return before, total


def scan_near(at_ref, got_ref, dt, out_ref, total_ref, step_ref, before_ref):
    index = at_ref[2]
    for m in range(0, ORDER, 2):
        steps = [jnp.exp(-float(ROWS) * row(dt, i)) for i in (m, m + 1)]
        before, total = scan_blocks(got_ref, m, steps, 8, index)
        for i in range(2):
            put(before_ref, m + i, before[i])
            put(step_ref, m + i, jnp.exp(-float(8 * ROWS) * row(dt, m + i)))
        both = jnp.concatenate(total, axis=0).astype(bf16)
        total_ref[m * GROUPS : (m + 2) * GROUPS, :] = both
        for copy in range(4):
            out_ref[(copy * ORDER + m) * GROUPS : (copy * ORDER + m + 2) * GROUPS, :] = both


def finish_lower(at_ref, far_ref, before_ref, dt, wt, *refs):
    st = refs[-3]
    near = at_ref[2].astype(f32)
    for m in range(ORDER):
        entry = row(before_ref, m) + jnp.exp(-float(ROWS) * near * row(dt, m)) * row(far_ref, m)
        put(st, m, row(wt, m) * entry)
    gate(dt, wt, *refs)


def finish_upper(at_ref, got_ref, half_ref, before_ref, dt, wt, *refs):
    st = refs[-3]
    place, place_f, near = at_ref[1], at_ref[1].astype(f32), at_ref[2].astype(f32)
    for m in range(0, ORDER, 2):
        rates = [row(dt, i) for i in (m, m + 1)]
        steps = [jnp.exp(-float(8 * ROWS) * d) for d in rates]
        far, _ = scan_blocks(got_ref, m, steps, 4, place)
        halves = load_pair(half_ref, 0, m)
        for i in range(2):
            far_i = far[i] + jnp.exp(-float(8 * ROWS) * place_f * rates[i]) * halves[i]
            entry = row(before_ref, m + i) + jnp.exp(-float(ROWS) * near * rates[i]) * far_i
            put(st, m + i, row(wt, m + i) * entry)
    gate(dt, wt, *refs)


def gate(
    dt, wt, skip_ref, qc_ref, g_ref, edge_ref, residual_ref, gain_ref,
    mixed_ref, scaled_ref, squares_ref, st, mt, sq,
):
    pole = [jnp.exp(-d) for d in rows_of(dt, ORDER)]
    skip = skip_ref[...]
    count = 16

    def block(n0, state, edge):
        state = list(state)
        for i in range(count):
            state = [p * s for p, s in zip(pole, state)]
            if i < edge:
                u = row(edge_ref, i)
                state = [s + row(wt, m) * u for m, s in enumerate(state)]
                value = row(edge_ref, 8 + i) * (skip * u + total_of(state))
            else:
                value = row(qc_ref, n0 + i) * (row(g_ref, n0 + i) + total_of(state))
            mt[i * GROUPS : (i + 1) * GROUPS, :] = value
        at = pl.ds(pl.multiple_of(n0, count), count)
        squares = None
        for j in range(GROUPS):
            lanes = slice(j * LANES, (j + 1) * LANES)
            tile = mt[pl.ds(j, count, stride=GROUPS), :].astype(bf16)
            mixed_ref[at, lanes] = tile
            summed = residual_ref[at, lanes].astype(f32) + tile.astype(f32)
            scaled_ref[at, lanes] = summed * gain_ref[0:1, lanes]
            part = summed * summed
            squares = part if squares is None else squares + part
        sq[at, :] = squares
        return tuple(state)

    state = block(0, rows_of(st, ORDER), TAPS - 1)
    lax.fori_loop(1, ROWS // count, lambda b, s: block(b * count, s, 0), state)
    squares_ref[...] = lax.dot_general(
        jnp.ones((8, LANES), f32), sq[...], (((1,), (1,)), ((), ())),
        precision=lax.Precision.HIGHEST, preferred_element_type=f32,
    )


def normalise(mixed_ref, scaled_ref, squares_ref, mixed_hbm, out_hbm, out, sems):
    first = pltpu.make_async_copy(mixed_ref, mixed_hbm, sems.at[0])
    first.start()
    total = lax.dot_general(
        squares_ref[...], jnp.ones((8, LANES), f32), (((0,), (0,)), ((), ())),
        precision=lax.Precision.HIGHEST, preferred_element_type=f32,
    )
    factor = lax.rsqrt(total / D + 1e-05)
    half = ROWS // 2
    copies = [first]
    for part in range(2):
        rows = slice(part * half, (part + 1) * half)
        for j in range(GROUPS):
            lanes = slice(j * LANES, (j + 1) * LANES)
            out[rows, lanes] = (scaled_ref[rows, lanes] * factor[rows]).astype(bf16)
        at = pl.ds(part * half, half)
        copy = pltpu.make_async_copy(out.at[at], out_hbm.at[at], sems.at[1 + part])
        copy.start()
        copies.append(copy)
    for copy in copies:
        copy.wait()


def shards(query, key, value, short_filter, residues, decay, skip_gain, residual, norm_gain):
    stacked = ((ROWS + 8) * GROUPS, LANES)
    modes = (ORDER * GROUPS, LANES)
    taps = (24 * GROUPS, LANES)
    blocks = (8 * ORDER * GROUPS, LANES)
    quads = (4 * ORDER * GROUPS, LANES)
    whole = (ROWS * GROUPS, LANES)
    natural = (ROWS, query.shape[1])
    vmem = pltpu.VMEM

    at = jnp.stack([lax.axis_index(name) for name in CONTEXT]).astype(jnp.int32)
    tails, q_here, k_here, v_here = call(
        fetch, "fetch", [((24, natural[1]), bf16)] + [(natural, bf16)] * 3, [pltpu.SemaphoreType.DMA((2, 3))],
        3, far=(0, 1, 2), limit=LIMIT,
    )(query, key, value)
    halo = lax.ppermute(tails, CONTEXT, [(i, i + 1) for i in range(63)])
    qc, own, clean, taps_t, heads, rates, weights, skip, gain = call(
        local_part, "local_part",
        [(whole, f32)] * 2 + [(modes, f32)] + [(taps, f32)] * 2 + [(modes, f32)] * 2
        + [((GROUPS, LANES), f32), ((1, natural[1]), f32)],
        [vmem(stacked, f32)] * 3 + [vmem(modes, f32)], 9, 1,
    )(at, q_here, k_here, v_here, short_filter, decay, residues, skip_gain[None], norm_gain[None])
    sent, edge = call(
        edge_part, "edge_part", [(blocks, bf16), ((16 * GROUPS, LANES), f32)], [vmem((48 * GROUPS, LANES), f32)], 5,
    )(halo, heads, taps_t, rates, clean)
    near = lax.all_to_all(sent, "y", 0, 0, tiled=True)
    quads_out, total, step, before = call(
        scan_near, "scan_near", [(quads, bf16), (modes, bf16), (modes, f32), (modes, f32)], [], 3, 1,
    )(at, near, rates)
    total, upper_half, place = lax.optimization_barrier((total, at[0], at[1]))
    z = 4 * upper_half + place
    even = lax.rem(z, 2) == 0

    def swapped(first):
        return lambda t, _: lax.ppermute(t, Z, [(first, first + 1), (first + 1, first)])

    def summed(mine, other):
        mine, other = mine.astype(f32), other.astype(f32)
        return step * jnp.where(even, mine, other) + jnp.where(even, other, mine)

    other = lax.cond(z < 2, swapped(0), lambda _, o: o, total, total)
    pair = summed(total, other).astype(bf16)
    arrived = lax.ppermute(pair, Z, [(0, 2), (1, 3)])
    total, pair = lax.optimization_barrier((total, pair))
    other = lax.cond((z == 2) | (z == 3), swapped(2), lambda _, o: o, total, other)
    arrived = arrived.astype(f32)
    four = (step * step * arrived + summed(total, other)).astype(bf16)
    carried = lax.ppermute(four, Z, [(2, 6), (3, 7)]), lax.ppermute(four, Z, [(2, 4), (3, 5)])
    far = jnp.where(even, arrived, step * arrived + other.astype(f32))
    quads_out, far, four = lax.optimization_barrier((quads_out, far, four))

    def finished(body, count, *own_args):
        mixed, scaled, squares = call(
            body, body.__name__,
            [(natural, bf16), (natural, f32), ((8, LANES), f32)],
            [vmem(modes, f32), vmem((16 * GROUPS, LANES), f32), vmem((ROWS, LANES), f32)],
            count, 1,
        )(at, *own_args, before, rates, weights, skip, qc, own, edge, residual, gain)
        return mixed, scaled, lax.all_to_all(squares, "tensor", 0, 0, tiled=True)

    def lower(_):
        return finished(finish_lower, 11, far), quads_out

    def upper(_):
        nothing = jnp.zeros(natural, bf16), jnp.zeros(natural, f32), jnp.zeros((8, LANES), f32)
        return nothing, lax.all_to_all(quads_out, "place", 0, 0, tiled=True)

    done, quad = lax.cond(z < 4, lower, upper, 0)
    carried = carried[0] + carried[1]
    mixed, scaled, gathered = lax.cond(
        z < 4, lambda d: d, lambda d: finished(finish_upper, 12, quad, carried), done
    )
    return call(
        normalise, "normalise", [(natural, bf16)] * 2, [vmem(natural, bf16), pltpu.SemaphoreType.DMA((3,))],
        3, far_out=True,
    )(mixed, scaled, gathered)


def solution(mesh):
    split = Mesh(mesh.devices.reshape(2, 4, 8, 8), CONTEXT + ("tensor",))
    rows = P(CONTEXT, "tensor")
    in_specs = (
        rows, rows, rows, P(None, None, "tensor"), P(None, "tensor"), P(None, "tensor"),
        P("tensor"), rows, P("tensor"),
    )
    return jax.shard_map(shards, mesh=split, in_specs=in_specs, out_specs=(rows, rows), check_vma=False)
```

```python
import jax
import jax.numpy as jnp
from jax import lax
from jax.experimental import pallas as pl
from jax.experimental.pallas import tpu as pltpu
from jax.sharding import Mesh, PartitionSpec as P

D = 8192
ORDER = 16
TAPS = 7
ROWS = 128
LANES = 128
GROUPS = 8
LIMIT = 54300 << 10
CONTEXT = ("half", "place", "y")
Z = CONTEXT[:2]
BLOCK = 8

f32 = jnp.float32
bf16 = jnp.bfloat16


def stack_rows(dst, src, first, rows, at, step=16):
    for r in range(0, rows, step):
        for j in range(GROUPS):
            tile = src[first + r : first + r + step, j * LANES : (j + 1) * LANES]
            dst[pl.ds((at + r) * GROUPS + j, step, stride=GROUPS), :] = tile.astype(f32)


def stack_taps(dst, taps, which):
    for j in range(GROUPS):
        dst[pl.ds(j, TAPS, stride=GROUPS), :] = taps[which, :, j * LANES : (j + 1) * LANES]


def row(ref, n):
    return ref[pl.ds(pl.multiple_of(n * GROUPS, GROUPS), GROUPS), :]


def put(ref, n, value):
    ref[pl.ds(pl.multiple_of(n * GROUPS, GROUPS), GROUPS), :] = value


def conv(ref, taps, n0, count):
    rows = [row(ref, n0 + 8 - (TAPS - 1) + i) for i in range(count + TAPS - 1)]
    out = []
    for i in range(count):
        total = rows[i + TAPS - 1] * taps[0]
        for j in range(1, TAPS):
            total = total + rows[i + TAPS - 1 - j] * taps[j]
        out.append(total)
    return out


def rows_of(ref, count):
    return [row(ref, m) for m in range(count)]


def total_of(values):
    values = list(values)
    while len(values) > 1:
        values = [a + b for a, b in zip(values[::2], values[1::2])] + (
            [values[-1]] if len(values) % 2 else []
        )
    return values[0]


def call(body, name, outs, scratch, count, scalars=0, far=(), limit=32 << 20, far_out=False):
    spec = pl.BlockSpec(memory_space=pltpu.VMEM)
    kinds = {i: pl.BlockSpec(memory_space=pltpu.SMEM) for i in range(scalars)}
    kinds.update({i: pl.BlockSpec(memory_space=pltpu.HBM) for i in far})
    return pl.pallas_call(
        body,
        name=name,
        out_shape=tuple(jax.ShapeDtypeStruct(s, t) for s, t in outs),
        in_specs=[kinds.get(i, spec) for i in range(count)],
        out_specs=tuple(pl.BlockSpec(memory_space=pltpu.HBM) if far_out else spec for _ in outs),
        scratch_shapes=scratch,
        compiler_params=pltpu.CompilerParams(vmem_limit_bytes=limit),
    )


def fetch(q_hbm, k_hbm, v_hbm, tails, q_out, k_out, v_out, sems):
    copies = []
    for i, (src, dst) in enumerate(((q_hbm, q_out), (k_hbm, k_out), (v_hbm, v_out))):
        ends = src.at[pl.ds(ROWS - 8, 8)], tails.at[pl.ds(8 * i, 8)]
        copies.append(pltpu.make_async_copy(*ends, sems.at[0, i]))
        copies.append(pltpu.make_async_copy(src, dst, sems.at[1, i]))
    for copy in copies[::2] + copies[1::2]:
        copy.start()
    for copy in copies:
        copy.wait()


def one_less_exp(d):
    square = d * d
    series = 1.0 + square / 72.0
    for divisor in (42.0, 20.0, 6.0):
        series = 1.0 + square * (1.0 / divisor) * series
    return 2.0 * jnp.exp(-d) * d * series


def local_part(
    at_ref, q_ref, k_ref, v_ref, f_ref, d_ref, r_ref, skip_ref, gain_ref,
    qc_ref, g_ref, state_ref, taps_ref, heads_ref, dt, wt, st, gain_out, qt, kt, vt, rt,
):
    del at_ref
    gain_out[...] = gain_ref[...]
    for i, (src, dst) in enumerate(((q_ref, qt), (k_ref, kt), (v_ref, vt))):
        stack_taps(taps_ref.at[pl.ds(8 * GROUPS * i, 8 * GROUPS)], f_ref, i)
        stack_rows(dst, src, 0, ROWS, 8)
        heads_ref[8 * GROUPS * i : 8 * GROUPS * (i + 1), :] = dst[8 * GROUPS : 16 * GROUPS, :]
    stack_rows(dt, d_ref, 0, ORDER, 0)
    stack_rows(rt, r_ref, 0, ORDER, 0)
    wt[...] = rt[...] * jnp.sqrt(one_less_exp(dt[...]))
    for j in range(GROUPS):
        st[j : j + 1, :] = skip_ref[0:1, j * LANES : (j + 1) * LANES]
    taps = [[row(taps_ref, 8 * i + j) for j in range(TAPS)] for i in range(3)]
    pole = [jnp.exp(-d) for d in rows_of(dt, ORDER)]
    skip = st[...]

    def block(n0, count, state):
        for i, c in enumerate(conv(qt, taps[0], n0, count)):
            put(qc_ref, n0 + i, c)
        us = [a * b for a, b in zip(conv(kt, taps[1], n0, count), conv(vt, taps[2], n0, count))]
        for i, u in enumerate(us):
            state = [u] * ORDER if state is None else [p * s + u for p, s in zip(pole, state)]
            terms = [row(wt, m) * s for m, s in enumerate(state)]
            put(g_ref, n0 + i, total_of(terms + [skip * u]))
        return state

    edge = TAPS - 1
    state = block(edge, BLOCK - edge, None)
    state = lax.fori_loop(
        1, ROWS // BLOCK, lambda b, s: tuple(block(b * BLOCK, BLOCK, list(s))), tuple(state)
    )
    for m in range(ORDER):
        put(state_ref, m, state[m])


def edge_part(halo_ref, heads_ref, taps_ref, dt, state_ref, out_ref, edge_ref, xt):
    edge = TAPS - 1
    convs = []
    for i in range(3):
        at = xt.at[pl.ds(16 * GROUPS * i, 16 * GROUPS)]
        stack_rows(at, halo_ref, 8 * i, 8, 0, 8)
        at[8 * GROUPS : 16 * GROUPS, :] = heads_ref[8 * GROUPS * i : 8 * GROUPS * (i + 1), :]
        convs.append(conv(at, [row(taps_ref, 8 * i + j) for j in range(TAPS)], 0, edge))
    us = [a * b for a, b in zip(convs[1], convs[2])]
    for i in range(edge):
        put(edge_ref, i, us[i])
        put(edge_ref, 8 + i, convs[0][i])
    for m in range(0, ORDER, 2):
        pair = []
        for i in (m, m + 1):
            d = row(dt, i)
            p = jnp.exp(-d)
            s = us[0]
            for u in us[1:]:
                s = p * s + u
            pair.append(row(state_ref, i) + jnp.exp(-(ROWS - edge) * d) * s)
        both = jnp.concatenate(pair, axis=0).astype(bf16)
        for copy in range(8):
            out_ref[(copy * ORDER + m) * GROUPS : (copy * ORDER + m + 2) * GROUPS, :] = both


def load_pair(ref, block, m):
    both = ref[(block * ORDER + m) * GROUPS : (block * ORDER + m + 2) * GROUPS, :].astype(f32)
    return both[:GROUPS], both[GROUPS:]


def scan_blocks(ref, m, steps, count, index=None):
    total = load_pair(ref, 0, m)
    before = [jnp.zeros_like(total[0])] * 2
    for b in range(1, count):
        if index is not None:
            before = [jnp.where(index == b, t, o) for t, o in zip(total, before)]
        total = [s * t + x for s, t, x in zip(steps, total, load_pair(ref, b, m))]
    return before, total


def scan_near(at_ref, got_ref, dt, out_ref, total_ref, step_ref, before_ref):
    index = at_ref[2]
    for m in range(0, ORDER, 2):
        steps = [jnp.exp(-float(ROWS) * row(dt, i)) for i in (m, m + 1)]
        before, total = scan_blocks(got_ref, m, steps, 8, index)
        for i in range(2):
            put(before_ref, m + i, before[i])
            put(step_ref, m + i, jnp.exp(-float(8 * ROWS) * row(dt, m + i)))
        both = jnp.concatenate(total, axis=0).astype(bf16)
        total_ref[m * GROUPS : (m + 2) * GROUPS, :] = both
        for copy in range(4):
            out_ref[(copy * ORDER + m) * GROUPS : (copy * ORDER + m + 2) * GROUPS, :] = both


def finish_lower(at_ref, far_ref, before_ref, dt, wt, *refs):
    st = refs[-3]
    near = at_ref[2].astype(f32)
    for m in range(ORDER):
        entry = row(before_ref, m) + jnp.exp(-float(ROWS) * near * row(dt, m)) * row(far_ref, m)
        put(st, m, row(wt, m) * entry)
    gate(dt, wt, *refs)


def finish_upper(at_ref, got_ref, half_ref, before_ref, dt, wt, *refs):
    st = refs[-3]
    place, place_f, near = at_ref[1], at_ref[1].astype(f32), at_ref[2].astype(f32)
    for m in range(0, ORDER, 2):
        rates = [row(dt, i) for i in (m, m + 1)]
        steps = [jnp.exp(-float(8 * ROWS) * d) for d in rates]
        far, _ = scan_blocks(got_ref, m, steps, 4, place)
        halves = load_pair(half_ref, 0, m)
        for i in range(2):
            far_i = far[i] + jnp.exp(-float(8 * ROWS) * place_f * rates[i]) * halves[i]
            entry = row(before_ref, m + i) + jnp.exp(-float(ROWS) * near * rates[i]) * far_i
            put(st, m + i, row(wt, m + i) * entry)
    gate(dt, wt, *refs)


def gate(
    dt, wt, skip_ref, qc_ref, g_ref, edge_ref, residual_ref, gain_ref,
    mixed_ref, scaled_ref, squares_ref, st, mt, sq,
):
    pole = [jnp.exp(-d) for d in rows_of(dt, ORDER)]
    skip = skip_ref[...]
    count = 16

    def block(n0, state, edge):
        state = list(state)
        for i in range(count):
            state = [p * s for p, s in zip(pole, state)]
            if i < edge:
                u = row(edge_ref, i)
                state = [s + row(wt, m) * u for m, s in enumerate(state)]
                value = row(edge_ref, 8 + i) * (skip * u + total_of(state))
            else:
                value = row(qc_ref, n0 + i) * (row(g_ref, n0 + i) + total_of(state))
            mt[i * GROUPS : (i + 1) * GROUPS, :] = value
        at = pl.ds(pl.multiple_of(n0, count), count)
        squares = None
        for j in range(GROUPS):
            lanes = slice(j * LANES, (j + 1) * LANES)
            tile = mt[pl.ds(j, count, stride=GROUPS), :].astype(bf16)
            mixed_ref[at, lanes] = tile
            summed = residual_ref[at, lanes].astype(f32) + tile.astype(f32)
            scaled_ref[at, lanes] = summed * gain_ref[0:1, lanes]
            part = summed * summed
            squares = part if squares is None else squares + part
        sq[at, :] = squares
        return tuple(state)

    state = block(0, rows_of(st, ORDER), TAPS - 1)
    lax.fori_loop(1, ROWS // count, lambda b, s: block(b * count, s, 0), state)
    squares_ref[...] = lax.dot_general(
        jnp.ones((8, LANES), f32), sq[...], (((1,), (1,)), ((), ())),
        precision=lax.Precision.HIGHEST, preferred_element_type=f32,
    )


def normalise(mixed_ref, scaled_ref, squares_ref, mixed_hbm, out_hbm, out, sems):
    first = pltpu.make_async_copy(mixed_ref, mixed_hbm, sems.at[0])
    first.start()
    total = lax.dot_general(
        squares_ref[...], jnp.ones((8, LANES), f32), (((0,), (0,)), ((), ())),
        precision=lax.Precision.HIGHEST, preferred_element_type=f32,
    )
    factor = lax.rsqrt(total / D + 1e-05)
    half = ROWS // 2
    copies = [first]
    for part in range(2):
        rows = slice(part * half, (part + 1) * half)
        for j in range(GROUPS):
            lanes = slice(j * LANES, (j + 1) * LANES)
            out[rows, lanes] = (scaled_ref[rows, lanes] * factor[rows]).astype(bf16)
        at = pl.ds(part * half, half)
        copy = pltpu.make_async_copy(out.at[at], out_hbm.at[at], sems.at[1 + part])
        copy.start()
        copies.append(copy)
    for copy in copies:
        copy.wait()


def shards(query, key, value, short_filter, residues, decay, skip_gain, residual, norm_gain):
    stacked = ((ROWS + 8) * GROUPS, LANES)
    modes = (ORDER * GROUPS, LANES)
    taps = (24 * GROUPS, LANES)
    blocks = (8 * ORDER * GROUPS, LANES)
    quads = (4 * ORDER * GROUPS, LANES)
    whole = (ROWS * GROUPS, LANES)
    natural = (ROWS, query.shape[1])
    vmem = pltpu.VMEM

    at = jnp.stack([lax.axis_index(name) for name in CONTEXT]).astype(jnp.int32)
    tails, q_here, k_here, v_here = call(
        fetch, "fetch", [((24, natural[1]), bf16)] + [(natural, bf16)] * 3, [pltpu.SemaphoreType.DMA((2, 3))],
        3, far=(0, 1, 2), limit=LIMIT,
    )(query, key, value)
    halo = lax.ppermute(tails, CONTEXT, [(i, i + 1) for i in range(63)])
    qc, own, clean, taps_t, heads, rates, weights, skip, gain = call(
        local_part, "local_part",
        [(whole, f32)] * 2 + [(modes, f32)] + [(taps, f32)] * 2 + [(modes, f32)] * 2
        + [((GROUPS, LANES), f32), ((1, natural[1]), f32)],
        [vmem(stacked, f32)] * 3 + [vmem(modes, f32)], 9, 1,
    )(at, q_here, k_here, v_here, short_filter, decay, residues, skip_gain[None], norm_gain[None])
    sent, edge = call(
        edge_part, "edge_part", [(blocks, bf16), ((16 * GROUPS, LANES), f32)], [vmem((48 * GROUPS, LANES), f32)], 5,
    )(halo, heads, taps_t, rates, clean)
    near = lax.all_to_all(sent, "y", 0, 0, tiled=True)
    quads_out, total, step, before = call(
        scan_near, "scan_near", [(quads, bf16), (modes, bf16), (modes, f32), (modes, f32)], [], 3, 1,
    )(at, near, rates)
    total, upper_half, place = lax.optimization_barrier((total, at[0], at[1]))
    z = 4 * upper_half + place
    even = lax.rem(z, 2) == 0

    def swapped(first):
        return lambda t, _: lax.ppermute(t, Z, [(first, first + 1), (first + 1, first)])

    def summed(mine, other):
        mine, other = mine.astype(f32), other.astype(f32)
        return step * jnp.where(even, mine, other) + jnp.where(even, other, mine)

    def by_pairs(total):
        other = lax.cond(z < 2, swapped(0), lambda _, o: o, total, total)
        pair = summed(total, other).astype(bf16)
        arrived = lax.ppermute(pair, Z, [(0, 2), (1, 3)])
        total, pair = lax.optimization_barrier((total, pair))
        other = lax.cond(z < 2, lambda _, o: o, swapped(2), total, other)
        arrived = arrived.astype(f32)
        four = (step * step * arrived + summed(total, other)).astype(bf16)
        return four, jnp.where(even, arrived, step * arrived + other.astype(f32))

    def unwritten(after, *outs):
        return call(lambda *_: None, "unwritten", outs, [], 1)(after)

    four, far = lax.cond(z < 4, by_pairs, lambda t: unwritten(t, (modes, bf16), (modes, f32)), total)
    carried = lax.ppermute(four, Z, [(2, 6), (3, 7)]), lax.ppermute(four, Z, [(2, 4), (3, 5)])
    quads_out, far, four = lax.optimization_barrier((quads_out, far, four))
    results = (natural, bf16), (natural, f32), ((8, LANES), f32)

    def finished(body, count, *own_args):
        mixed, scaled, squares = call(
            body, body.__name__, results,
            [vmem(modes, f32), vmem((16 * GROUPS, LANES), f32), vmem((ROWS, LANES), f32)],
            count, 1,
        )(at, *own_args, before, rates, weights, skip, qc, own, edge, residual, gain)
        return mixed, scaled, lax.all_to_all(squares, "tensor", 0, 0, tiled=True)

    def lower(_):
        done = finished(finish_lower, 11, far)
        return *done, *unwritten(done[2], (quads, bf16))

    def upper(_):
        quad = lax.all_to_all(quads_out, "place", 0, 0, tiled=True)
        return *unwritten(quad, *results), quad

    *done, quad = lax.cond(z < 4, lower, upper, 0)
    carried = carried[0] + carried[1]
    mixed, scaled, gathered = lax.cond(
        z < 4, lambda d: d, lambda _: finished(finish_upper, 12, quad, carried), tuple(done)
    )
    return call(
        normalise, "normalise", [(natural, bf16)] * 2, [vmem(natural, bf16), pltpu.SemaphoreType.DMA((3,))],
        3, far_out=True,
    )(mixed, scaled, gathered)


def solution(mesh):
    split = Mesh(mesh.devices.reshape(2, 4, 8, 8), CONTEXT + ("tensor",))
    rows = P(CONTEXT, "tensor")
    in_specs = (
        rows, rows, rows, P(None, None, "tensor"), P(None, "tensor"), P(None, "tensor"),
        P("tensor"), rows, P("tensor"),
    )
    return jax.shard_map(shards, mesh=split, in_specs=in_specs, out_specs=(rows, rows), check_vma=False)
```

```python
import jax
import jax.numpy as jnp
from jax import lax
from jax.experimental import pallas as pl
from jax.experimental.pallas import tpu as pltpu
from jax.sharding import Mesh, PartitionSpec as P

D = 8192
ORDER = 16
TAPS = 7
ROWS = 128
LANES = 128
GROUPS = 8
LIMIT = 54300 << 10
CONTEXT = ("half", "place", "y")
Z = CONTEXT[:2]
BLOCK = 8

f32 = jnp.float32
bf16 = jnp.bfloat16


def stack_rows(dst, src, first, rows, at, step=16):
    for r in range(0, rows, step):
        for j in range(GROUPS):
            tile = src[first + r : first + r + step, j * LANES : (j + 1) * LANES]
            dst[pl.ds((at + r) * GROUPS + j, step, stride=GROUPS), :] = tile.astype(f32)


def stack_taps(dst, taps, which):
    for j in range(GROUPS):
        dst[pl.ds(j, TAPS, stride=GROUPS), :] = taps[which, :, j * LANES : (j + 1) * LANES]


def row(ref, n):
    return ref[pl.ds(pl.multiple_of(n * GROUPS, GROUPS), GROUPS), :]


def put(ref, n, value):
    ref[pl.ds(pl.multiple_of(n * GROUPS, GROUPS), GROUPS), :] = value


def conv(ref, taps, n0, count):
    rows = [row(ref, n0 + 8 - (TAPS - 1) + i) for i in range(count + TAPS - 1)]
    out = []
    for i in range(count):
        total = rows[i + TAPS - 1] * taps[0]
        for j in range(1, TAPS):
            total = total + rows[i + TAPS - 1 - j] * taps[j]
        out.append(total)
    return out


def rows_of(ref, count):
    return [row(ref, m) for m in range(count)]


def total_of(values):
    values = list(values)
    while len(values) > 1:
        values = [a + b for a, b in zip(values[::2], values[1::2])] + (
            [values[-1]] if len(values) % 2 else []
        )
    return values[0]


def call(body, name, outs, scratch, count, scalars=0, far=(), limit=32 << 20, far_out=False):
    spec = pl.BlockSpec(memory_space=pltpu.VMEM)
    kinds = {i: pl.BlockSpec(memory_space=pltpu.SMEM) for i in range(scalars)}
    kinds.update({i: pl.BlockSpec(memory_space=pltpu.HBM) for i in far})
    return pl.pallas_call(
        body,
        name=name,
        out_shape=tuple(jax.ShapeDtypeStruct(s, t) for s, t in outs),
        in_specs=[kinds.get(i, spec) for i in range(count)],
        out_specs=tuple(pl.BlockSpec(memory_space=pltpu.HBM) if far_out else spec for _ in outs),
        scratch_shapes=scratch,
        compiler_params=pltpu.CompilerParams(vmem_limit_bytes=limit),
    )


def fetch(q_hbm, k_hbm, v_hbm, tails, q_out, k_out, v_out, sems):
    copies = []
    for i, (src, dst) in enumerate(((q_hbm, q_out), (k_hbm, k_out), (v_hbm, v_out))):
        ends = src.at[pl.ds(ROWS - 8, 8)], tails.at[pl.ds(8 * i, 8)]
        copies.append(pltpu.make_async_copy(*ends, sems.at[0, i]))
        copies.append(pltpu.make_async_copy(src, dst, sems.at[1, i]))
    for copy in copies[::2] + copies[1::2]:
        copy.start()
    for copy in copies:
        copy.wait()


def one_less_exp(d):
    square = d * d
    series = 1.0 + square / 72.0
    for divisor in (42.0, 20.0, 6.0):
        series = 1.0 + square * (1.0 / divisor) * series
    return 2.0 * jnp.exp(-d) * d * series


def local_part(
    at_ref, q_ref, k_ref, v_ref, f_ref, d_ref, r_ref, skip_ref, gain_ref,
    qc_ref, g_ref, state_ref, taps_ref, heads_ref, dt, wt, st, gain_out, qt, kt, vt, rt,
):
    del at_ref
    gain_out[...] = gain_ref[...]
    for i, (src, dst) in enumerate(((q_ref, qt), (k_ref, kt), (v_ref, vt))):
        stack_taps(taps_ref.at[pl.ds(8 * GROUPS * i, 8 * GROUPS)], f_ref, i)
        stack_rows(dst, src, 0, ROWS, 8)
        heads_ref[8 * GROUPS * i : 8 * GROUPS * (i + 1), :] = dst[8 * GROUPS : 16 * GROUPS, :]
    stack_rows(dt, d_ref, 0, ORDER, 0)
    stack_rows(rt, r_ref, 0, ORDER, 0)
    wt[...] = rt[...] * jnp.sqrt(one_less_exp(dt[...]))
    for j in range(GROUPS):
        st[j : j + 1, :] = skip_ref[0:1, j * LANES : (j + 1) * LANES]
    taps = [[row(taps_ref, 8 * i + j) for j in range(TAPS)] for i in range(3)]
    pole = [jnp.exp(-d) for d in rows_of(dt, ORDER)]
    skip = st[...]

    def block(n0, count, state):
        for i, c in enumerate(conv(qt, taps[0], n0, count)):
            put(qc_ref, n0 + i, c)
        us = [a * b for a, b in zip(conv(kt, taps[1], n0, count), conv(vt, taps[2], n0, count))]
        for i, u in enumerate(us):
            state = [u] * ORDER if state is None else [p * s + u for p, s in zip(pole, state)]
            terms = [row(wt, m) * s for m, s in enumerate(state)]
            put(g_ref, n0 + i, total_of(terms + [skip * u]))
        return state

    edge = TAPS - 1
    state = block(edge, BLOCK - edge, None)
    state = lax.fori_loop(
        1, ROWS // BLOCK, lambda b, s: tuple(block(b * BLOCK, BLOCK, list(s))), tuple(state)
    )
    for m in range(ORDER):
        put(state_ref, m, state[m])


def edge_part(halo_ref, heads_ref, taps_ref, dt, state_ref, out_ref, edge_ref, xt):
    edge = TAPS - 1
    convs = []
    for i in range(3):
        at = xt.at[pl.ds(16 * GROUPS * i, 16 * GROUPS)]
        stack_rows(at, halo_ref, 8 * i, 8, 0, 8)
        at[8 * GROUPS : 16 * GROUPS, :] = heads_ref[8 * GROUPS * i : 8 * GROUPS * (i + 1), :]
        convs.append(conv(at, [row(taps_ref, 8 * i + j) for j in range(TAPS)], 0, edge))
    us = [a * b for a, b in zip(convs[1], convs[2])]
    for i in range(edge):
        put(edge_ref, i, us[i])
        put(edge_ref, 8 + i, convs[0][i])
    for m in range(0, ORDER, 2):
        pair = []
        for i in (m, m + 1):
            d = row(dt, i)
            p = jnp.exp(-d)
            s = us[0]
            for u in us[1:]:
                s = p * s + u
            pair.append(row(state_ref, i) + jnp.exp(-(ROWS - edge) * d) * s)
        both = jnp.concatenate(pair, axis=0).astype(bf16)
        for copy in range(8):
            out_ref[(copy * ORDER + m) * GROUPS : (copy * ORDER + m + 2) * GROUPS, :] = both


def load_pair(ref, block, m):
    both = ref[(block * ORDER + m) * GROUPS : (block * ORDER + m + 2) * GROUPS, :].astype(f32)
    return both[:GROUPS], both[GROUPS:]


def scan_blocks(ref, m, steps, count, index=None):
    total = load_pair(ref, 0, m)
    before = [jnp.zeros_like(total[0])] * 2
    for b in range(1, count):
        if index is not None:
            before = [jnp.where(index == b, t, o) for t, o in zip(total, before)]
        total = [s * t + x for s, t, x in zip(steps, total, load_pair(ref, b, m))]
    return before, total


def scan_near(at_ref, got_ref, dt, out_ref, total_ref, step_ref, before_ref):
    index = at_ref[2]
    for m in range(0, ORDER, 2):
        steps = [jnp.exp(-float(ROWS) * row(dt, i)) for i in (m, m + 1)]
        before, total = scan_blocks(got_ref, m, steps, 8, index)
        for i in range(2):
            put(before_ref, m + i, before[i])
            put(step_ref, m + i, jnp.exp(-float(8 * ROWS) * row(dt, m + i)))
        both = jnp.concatenate(total, axis=0).astype(bf16)
        total_ref[m * GROUPS : (m + 2) * GROUPS, :] = both
        for copy in range(4):
            out_ref[(copy * ORDER + m) * GROUPS : (copy * ORDER + m + 2) * GROUPS, :] = both


def finish_lower(at_ref, far_ref, before_ref, dt, wt, *refs):
    st = refs[-3]
    near = at_ref[2].astype(f32)
    for m in range(ORDER):
        entry = row(before_ref, m) + jnp.exp(-float(ROWS) * near * row(dt, m)) * row(far_ref, m)
        put(st, m, row(wt, m) * entry)
    gate(dt, wt, *refs)


def finish_upper(at_ref, got_ref, half_ref, before_ref, dt, wt, *refs):
    st = refs[-3]
    place, place_f, near = at_ref[1], at_ref[1].astype(f32), at_ref[2].astype(f32)
    for m in range(0, ORDER, 2):
        rates = [row(dt, i) for i in (m, m + 1)]
        steps = [jnp.exp(-float(8 * ROWS) * d) for d in rates]
        far, _ = scan_blocks(got_ref, m, steps, 4, place)
        halves = load_pair(half_ref, 0, m)
        for i in range(2):
            far_i = far[i] + jnp.exp(-float(8 * ROWS) * place_f * rates[i]) * halves[i]
            entry = row(before_ref, m + i) + jnp.exp(-float(ROWS) * near * rates[i]) * far_i
            put(st, m + i, row(wt, m + i) * entry)
    gate(dt, wt, *refs)


def gate(
    dt, wt, skip_ref, qc_ref, g_ref, edge_ref, residual_ref, gain_ref,
    mixed_ref, scaled_ref, squares_ref, st, mt, sq,
):
    pole = [jnp.exp(-d) for d in rows_of(dt, ORDER)]
    skip = skip_ref[...]
    count = 16

    def block(n0, state, edge):
        state = list(state)
        for i in range(count):
            state = [p * s for p, s in zip(pole, state)]
            if i < edge:
                u = row(edge_ref, i)
                state = [s + row(wt, m) * u for m, s in enumerate(state)]
                value = row(edge_ref, 8 + i) * (skip * u + total_of(state))
            else:
                value = row(qc_ref, n0 + i) * (row(g_ref, n0 + i) + total_of(state))
            mt[i * GROUPS : (i + 1) * GROUPS, :] = value
        at = pl.ds(pl.multiple_of(n0, count), count)
        squares = None
        for j in range(GROUPS):
            lanes = slice(j * LANES, (j + 1) * LANES)
            tile = mt[pl.ds(j, count, stride=GROUPS), :].astype(bf16)
            mixed_ref[at, lanes] = tile
            summed = residual_ref[at, lanes].astype(f32) + tile.astype(f32)
            scaled_ref[at, lanes] = summed * gain_ref[0:1, lanes]
            part = summed * summed
            squares = part if squares is None else squares + part
        sq[at, :] = squares
        return tuple(state)

    state = block(0, rows_of(st, ORDER), TAPS - 1)
    lax.fori_loop(1, ROWS // count, lambda b, s: block(b * count, s, 0), state)
    squares_ref[...] = lax.dot_general(
        jnp.ones((8, LANES), f32), sq[...], (((1,), (1,)), ((), ())),
        precision=lax.Precision.HIGHEST, preferred_element_type=f32,
    )


def normalise(mixed_ref, scaled_ref, squares_ref, mixed_hbm, out_hbm, out, sems):
    first = pltpu.make_async_copy(mixed_ref, mixed_hbm, sems.at[0])
    first.start()
    total = lax.dot_general(
        squares_ref[...], jnp.ones((8, LANES), f32), (((0,), (0,)), ((), ())),
        precision=lax.Precision.HIGHEST, preferred_element_type=f32,
    )
    factor = lax.rsqrt(total / D + 1e-05)
    half = ROWS // 2
    copies = [first]
    for part in range(2):
        rows = slice(part * half, (part + 1) * half)
        for j in range(GROUPS):
            lanes = slice(j * LANES, (j + 1) * LANES)
            out[rows, lanes] = (scaled_ref[rows, lanes] * factor[rows]).astype(bf16)
        at = pl.ds(part * half, half)
        copy = pltpu.make_async_copy(out.at[at], out_hbm.at[at], sems.at[1 + part])
        copy.start()
        copies.append(copy)
    for copy in copies:
        copy.wait()


def shards(query, key, value, short_filter, residues, decay, skip_gain, residual, norm_gain):
    stacked = ((ROWS + 8) * GROUPS, LANES)
    modes = (ORDER * GROUPS, LANES)
    taps = (24 * GROUPS, LANES)
    blocks = (8 * ORDER * GROUPS, LANES)
    quads = (4 * ORDER * GROUPS, LANES)
    whole = (ROWS * GROUPS, LANES)
    natural = (ROWS, query.shape[1])
    vmem = pltpu.VMEM

    at = jnp.stack([lax.axis_index(name) for name in CONTEXT]).astype(jnp.int32)
    tails, q_here, k_here, v_here = call(
        fetch, "fetch", [((24, natural[1]), bf16)] + [(natural, bf16)] * 3, [pltpu.SemaphoreType.DMA((2, 3))],
        3, far=(0, 1, 2), limit=LIMIT,
    )(query, key, value)
    halo = lax.ppermute(tails, CONTEXT, [(i, i + 1) for i in range(63)])
    qc, own, clean, taps_t, heads, rates, weights, skip, gain = call(
        local_part, "local_part",
        [(whole, f32)] * 2 + [(modes, f32)] + [(taps, f32)] * 2 + [(modes, f32)] * 2
        + [((GROUPS, LANES), f32), ((1, natural[1]), f32)],
        [vmem(stacked, f32)] * 3 + [vmem(modes, f32)], 9, 1,
    )(at, q_here, k_here, v_here, short_filter, decay, residues, skip_gain[None], norm_gain[None])
    sent, edge = call(
        edge_part, "edge_part", [(blocks, bf16), ((16 * GROUPS, LANES), f32)], [vmem((48 * GROUPS, LANES), f32)], 5,
    )(halo, heads, taps_t, rates, clean)
    near = lax.all_to_all(sent, "y", 0, 0, tiled=True)
    quads_out, total, step, before = call(
        scan_near, "scan_near", [(quads, bf16), (modes, bf16), (modes, f32), (modes, f32)], [], 3, 1,
    )(at, near, rates)
    total, upper_half, place = lax.optimization_barrier((total, at[0], at[1]))
    z = 4 * upper_half + place
    even = lax.rem(z, 2) == 0

    def swapped(first):
        return lambda t, _: lax.ppermute(t, Z, [(first, first + 1), (first + 1, first)])

    def summed(mine, other):
        mine, other = mine.astype(f32), other.astype(f32)
        return step * jnp.where(even, mine, other) + jnp.where(even, other, mine)

    def by_pairs(total):
        other = lax.cond(z < 2, swapped(0), lambda _, o: o, total, total)
        pair = summed(total, other).astype(bf16)
        arrived = lax.ppermute(pair, Z, [(0, 2), (1, 3)])
        total, pair = lax.optimization_barrier((total, pair))
        other = lax.cond(z < 2, lambda _, o: o, swapped(2), total, other)
        arrived = arrived.astype(f32)
        four = (step * step * arrived + summed(total, other)).astype(bf16)
        return four, jnp.where(even, arrived, step * arrived + other.astype(f32))

    def unwritten(after, *outs):
        return call(lambda *_: None, "unwritten", outs, [], 1)(after)

    four, far = lax.cond(z < 4, by_pairs, lambda t: unwritten(t, (modes, bf16), (modes, f32)), total)
    carried = lax.ppermute(four, Z, [(2, 6), (3, 7)]), lax.ppermute(four, Z, [(2, 4), (3, 5)])
    quads_out, far, four = lax.optimization_barrier((quads_out, far, four))
    results = (natural, bf16), (natural, f32), ((8, LANES), f32)

    def finished(body, count, *own_args):
        return call(
            body, body.__name__, results,
            [vmem(modes, f32), vmem((16 * GROUPS, LANES), f32), vmem((ROWS, LANES), f32)],
            count, 1,
        )(at, *own_args, before, rates, weights, skip, qc, own, edge, residual, gain)

    def lower(_):
        done = finished(finish_lower, 11, far)
        return *done, *unwritten(far, (quads, bf16))

    def upper(_):
        quad = lax.all_to_all(quads_out, "place", 0, 0, tiled=True)
        return *unwritten(quad, *results), quad

    *done, quad = lax.cond(z < 4, lower, upper, 0)
    carried = carried[0] + carried[1]
    mixed, scaled, squares = lax.cond(
        z < 4, lambda d: d, lambda _: finished(finish_upper, 12, quad, carried), tuple(done)
    )
    gathered = lax.all_to_all(squares, "tensor", 0, 0, tiled=True)
    return call(
        normalise, "normalise", [(natural, bf16)] * 2, [vmem(natural, bf16), pltpu.SemaphoreType.DMA((3,))],
        3, far_out=True,
    )(mixed, scaled, gathered)


def solution(mesh):
    split = Mesh(mesh.devices.reshape(2, 4, 8, 8), CONTEXT + ("tensor",))
    rows = P(CONTEXT, "tensor")
    in_specs = (
        rows, rows, rows, P(None, None, "tensor"), P(None, "tensor"), P(None, "tensor"),
        P("tensor"), rows, P("tensor"),
    )
    return jax.shard_map(shards, mesh=split, in_specs=in_specs, out_specs=(rows, rows), check_vma=False)
```

```python
import jax
import jax.numpy as jnp
from jax import lax
from jax.experimental import pallas as pl
from jax.experimental.pallas import tpu as pltpu
from jax.sharding import Mesh, PartitionSpec as P

D = 8192
ORDER = 16
TAPS = 7
ROWS = 128
LANES = 128
GROUPS = 8
LIMIT = 54300 << 10
CONTEXT = ("half", "place", "y")
Z = CONTEXT[:2]
BLOCK = 8

f32 = jnp.float32
bf16 = jnp.bfloat16


def stack_rows(dst, src, first, rows, at, step=16):
    for r in range(0, rows, step):
        for j in range(GROUPS):
            tile = src[first + r : first + r + step, j * LANES : (j + 1) * LANES]
            dst[pl.ds((at + r) * GROUPS + j, step, stride=GROUPS), :] = tile.astype(f32)


def stack_taps(dst, taps, which):
    for j in range(GROUPS):
        dst[pl.ds(j, TAPS, stride=GROUPS), :] = taps[which, :, j * LANES : (j + 1) * LANES]


def row(ref, n):
    return ref[pl.ds(pl.multiple_of(n * GROUPS, GROUPS), GROUPS), :]


def put(ref, n, value):
    ref[pl.ds(pl.multiple_of(n * GROUPS, GROUPS), GROUPS), :] = value


def conv(ref, taps, n0, count):
    rows = [row(ref, n0 + 8 - (TAPS - 1) + i) for i in range(count + TAPS - 1)]
    out = []
    for i in range(count):
        total = rows[i + TAPS - 1] * taps[0]
        for j in range(1, TAPS):
            total = total + rows[i + TAPS - 1 - j] * taps[j]
        out.append(total)
    return out


def rows_of(ref, count):
    return [row(ref, m) for m in range(count)]


def total_of(values):
    values = list(values)
    while len(values) > 1:
        values = [a + b for a, b in zip(values[::2], values[1::2])] + (
            [values[-1]] if len(values) % 2 else []
        )
    return values[0]


def call(body, name, outs, scratch, count, scalars=0, far=(), limit=32 << 20, far_out=False):
    spec = pl.BlockSpec(memory_space=pltpu.VMEM)
    kinds = {i: pl.BlockSpec(memory_space=pltpu.SMEM) for i in range(scalars)}
    kinds.update({i: pl.BlockSpec(memory_space=pltpu.HBM) for i in far})
    return pl.pallas_call(
        body,
        name=name,
        out_shape=tuple(jax.ShapeDtypeStruct(s, t) for s, t in outs),
        in_specs=[kinds.get(i, spec) for i in range(count)],
        out_specs=tuple(pl.BlockSpec(memory_space=pltpu.HBM) if far_out else spec for _ in outs),
        scratch_shapes=scratch,
        compiler_params=pltpu.CompilerParams(vmem_limit_bytes=limit),
    )


def fetch(q_hbm, k_hbm, v_hbm, tails, q_out, k_out, v_out, sems):
    copies = []
    for i, (src, dst) in enumerate(((q_hbm, q_out), (k_hbm, k_out), (v_hbm, v_out))):
        ends = src.at[pl.ds(ROWS - 8, 8)], tails.at[pl.ds(8 * i, 8)]
        copies.append(pltpu.make_async_copy(*ends, sems.at[0, i]))
        copies.append(pltpu.make_async_copy(src, dst, sems.at[1, i]))
    for copy in copies[::2] + copies[1::2]:
        copy.start()
    for copy in copies:
        copy.wait()


def one_less_exp(d):
    square = d * d
    series = 1.0 + square / 72.0
    for divisor in (42.0, 20.0, 6.0):
        series = 1.0 + square * (1.0 / divisor) * series
    return 2.0 * jnp.exp(-d) * d * series


def local_part(
    at_ref, q_ref, k_ref, v_ref, f_ref, d_ref, r_ref, skip_ref, gain_ref,
    qc_ref, g_ref, state_ref, taps_ref, heads_ref, dt, wt, st, gain_out, qt, kt, vt, rt,
):
    del at_ref
    gain_out[...] = gain_ref[...]
    for i, (src, dst) in enumerate(((q_ref, qt), (k_ref, kt), (v_ref, vt))):
        stack_taps(taps_ref.at[pl.ds(8 * GROUPS * i, 8 * GROUPS)], f_ref, i)
        stack_rows(dst, src, 0, ROWS, 8)
        heads_ref[8 * GROUPS * i : 8 * GROUPS * (i + 1), :] = dst[8 * GROUPS : 16 * GROUPS, :]
    stack_rows(dt, d_ref, 0, ORDER, 0)
    stack_rows(rt, r_ref, 0, ORDER, 0)
    wt[...] = rt[...] * jnp.sqrt(one_less_exp(dt[...]))
    for j in range(GROUPS):
        st[j : j + 1, :] = skip_ref[0:1, j * LANES : (j + 1) * LANES]
    taps = [[row(taps_ref, 8 * i + j) for j in range(TAPS)] for i in range(3)]
    pole = [jnp.exp(-d) for d in rows_of(dt, ORDER)]
    skip = st[...]

    def block(n0, count, state):
        for i, c in enumerate(conv(qt, taps[0], n0, count)):
            put(qc_ref, n0 + i, c)
        us = [a * b for a, b in zip(conv(kt, taps[1], n0, count), conv(vt, taps[2], n0, count))]
        for i, u in enumerate(us):
            state = [u] * ORDER if state is None else [p * s + u for p, s in zip(pole, state)]
            terms = [row(wt, m) * s for m, s in enumerate(state)]
            put(g_ref, n0 + i, total_of(terms + [skip * u]))
        return state

    edge = TAPS - 1
    state = block(edge, BLOCK - edge, None)
    state = lax.fori_loop(
        1, ROWS // BLOCK, lambda b, s: tuple(block(b * BLOCK, BLOCK, list(s))), tuple(state)
    )
    for m in range(ORDER):
        put(state_ref, m, state[m])


def edge_part(halo_ref, heads_ref, taps_ref, dt, state_ref, out_ref, edge_ref, xt):
    edge = TAPS - 1
    convs = []
    for i in range(3):
        at = xt.at[pl.ds(16 * GROUPS * i, 16 * GROUPS)]
        stack_rows(at, halo_ref, 8 * i, 8, 0, 8)
        at[8 * GROUPS : 16 * GROUPS, :] = heads_ref[8 * GROUPS * i : 8 * GROUPS * (i + 1), :]
        convs.append(conv(at, [row(taps_ref, 8 * i + j) for j in range(TAPS)], 0, edge))
    us = [a * b for a, b in zip(convs[1], convs[2])]
    for i in range(edge):
        put(edge_ref, i, us[i])
        put(edge_ref, 8 + i, convs[0][i])
    for m in range(0, ORDER, 2):
        pair = []
        for i in (m, m + 1):
            d = row(dt, i)
            p = jnp.exp(-d)
            s = us[0]
            for u in us[1:]:
                s = p * s + u
            pair.append(row(state_ref, i) + jnp.exp(-(ROWS - edge) * d) * s)
        both = jnp.concatenate(pair, axis=0).astype(bf16)
        for copy in range(8):
            out_ref[(copy * ORDER + m) * GROUPS : (copy * ORDER + m + 2) * GROUPS, :] = both


def load_pair(ref, block, m):
    both = ref[(block * ORDER + m) * GROUPS : (block * ORDER + m + 2) * GROUPS, :].astype(f32)
    return both[:GROUPS], both[GROUPS:]


def scan_blocks(ref, m, steps, count, index=None):
    total = load_pair(ref, 0, m)
    before = [jnp.zeros_like(total[0])] * 2
    for b in range(1, count):
        if index is not None:
            before = [jnp.where(index == b, t, o) for t, o in zip(total, before)]
        total = [s * t + x for s, t, x in zip(steps, total, load_pair(ref, b, m))]
    return before, total


def scan_near(at_ref, got_ref, dt, out_ref, total_ref, step_ref, before_ref):
    index = at_ref[2]
    for m in range(0, ORDER, 2):
        steps = [jnp.exp(-float(ROWS) * row(dt, i)) for i in (m, m + 1)]
        before, total = scan_blocks(got_ref, m, steps, 8, index)
        for i in range(2):
            put(before_ref, m + i, before[i])
            put(step_ref, m + i, jnp.exp(-float(8 * ROWS) * row(dt, m + i)))
        both = jnp.concatenate(total, axis=0).astype(bf16)
        total_ref[m * GROUPS : (m + 2) * GROUPS, :] = both
        for copy in range(4):
            out_ref[(copy * ORDER + m) * GROUPS : (copy * ORDER + m + 2) * GROUPS, :] = both


def finish_lower(at_ref, far_ref, before_ref, dt, wt, *refs):
    st = refs[-3]
    near = at_ref[2].astype(f32)
    for m in range(ORDER):
        entry = row(before_ref, m) + jnp.exp(-float(ROWS) * near * row(dt, m)) * row(far_ref, m)
        put(st, m, row(wt, m) * entry)
    gate(dt, wt, *refs)


def finish_upper(at_ref, got_ref, half_ref, before_ref, dt, wt, *refs):
    st = refs[-3]
    place, place_f, near = at_ref[1], at_ref[1].astype(f32), at_ref[2].astype(f32)
    for m in range(0, ORDER, 2):
        rates = [row(dt, i) for i in (m, m + 1)]
        steps = [jnp.exp(-float(8 * ROWS) * d) for d in rates]
        far, _ = scan_blocks(got_ref, m, steps, 4, place)
        halves = load_pair(half_ref, 0, m)
        for i in range(2):
            far_i = far[i] + jnp.exp(-float(8 * ROWS) * place_f * rates[i]) * halves[i]
            entry = row(before_ref, m + i) + jnp.exp(-float(ROWS) * near * rates[i]) * far_i
            put(st, m + i, row(wt, m + i) * entry)
    gate(dt, wt, *refs)


def gate(
    dt, wt, skip_ref, qc_ref, g_ref, edge_ref, residual_ref, gain_ref,
    mixed_ref, scaled_ref, squares_ref, st, mt, sq,
):
    pole = [jnp.exp(-d) for d in rows_of(dt, ORDER)]
    skip = skip_ref[...]
    count = 16

    def block(n0, state, edge):
        state = list(state)
        for i in range(count):
            state = [p * s for p, s in zip(pole, state)]
            if i < edge:
                u = row(edge_ref, i)
                state = [s + row(wt, m) * u for m, s in enumerate(state)]
                value = row(edge_ref, 8 + i) * (skip * u + total_of(state))
            else:
                value = row(qc_ref, n0 + i) * (row(g_ref, n0 + i) + total_of(state))
            mt[i * GROUPS : (i + 1) * GROUPS, :] = value
        at = pl.ds(pl.multiple_of(n0, count), count)
        squares = None
        for j in range(GROUPS):
            lanes = slice(j * LANES, (j + 1) * LANES)
            tile = mt[pl.ds(j, count, stride=GROUPS), :].astype(bf16)
            mixed_ref[at, lanes] = tile
            summed = residual_ref[at, lanes].astype(f32) + tile.astype(f32)
            scaled_ref[at, lanes] = summed * gain_ref[0:1, lanes]
            part = summed * summed
            squares = part if squares is None else squares + part
        sq[at, :] = squares
        return tuple(state)

    state = block(0, rows_of(st, ORDER), TAPS - 1)
    lax.fori_loop(1, ROWS // count, lambda b, s: block(b * count, s, 0), state)
    squares_ref[...] = lax.dot_general(
        jnp.ones((8, LANES), f32), sq[...], (((1,), (1,)), ((), ())),
        precision=lax.Precision.HIGHEST, preferred_element_type=f32,
    )


def normalise(mixed_ref, scaled_ref, squares_ref, mixed_hbm, out_hbm, out, sems):
    first = pltpu.make_async_copy(mixed_ref, mixed_hbm, sems.at[0])
    first.start()
    total = lax.dot_general(
        squares_ref[...], jnp.ones((8, LANES), f32), (((0,), (0,)), ((), ())),
        precision=lax.Precision.HIGHEST, preferred_element_type=f32,
    )
    factor = lax.rsqrt(total / D + 1e-05)
    half = ROWS // 2
    copies = [first]
    for part in range(2):
        rows = slice(part * half, (part + 1) * half)
        for j in range(GROUPS):
            lanes = slice(j * LANES, (j + 1) * LANES)
            out[rows, lanes] = (scaled_ref[rows, lanes] * factor[rows]).astype(bf16)
        at = pl.ds(part * half, half)
        copy = pltpu.make_async_copy(out.at[at], out_hbm.at[at], sems.at[1 + part])
        copy.start()
        copies.append(copy)
    for copy in copies:
        copy.wait()


def shards(query, key, value, short_filter, residues, decay, skip_gain, residual, norm_gain):
    stacked = ((ROWS + 8) * GROUPS, LANES)
    modes = (ORDER * GROUPS, LANES)
    taps = (24 * GROUPS, LANES)
    blocks = (8 * ORDER * GROUPS, LANES)
    quads = (4 * ORDER * GROUPS, LANES)
    whole = (ROWS * GROUPS, LANES)
    natural = (ROWS, query.shape[1])
    vmem = pltpu.VMEM

    at = jnp.stack([lax.axis_index(name) for name in CONTEXT]).astype(jnp.int32)
    tails, q_here, k_here, v_here = call(
        fetch, "fetch", [((24, natural[1]), bf16)] + [(natural, bf16)] * 3, [pltpu.SemaphoreType.DMA((2, 3))],
        3, far=(0, 1, 2), limit=LIMIT,
    )(query, key, value)
    halo = lax.ppermute(tails, CONTEXT, [(i, i + 1) for i in range(63)])
    qc, own, clean, taps_t, heads, rates, weights, skip, gain = call(
        local_part, "local_part",
        [(whole, f32)] * 2 + [(modes, f32)] + [(taps, f32)] * 2 + [(modes, f32)] * 2
        + [((GROUPS, LANES), f32), ((1, natural[1]), f32)],
        [vmem(stacked, f32)] * 3 + [vmem(modes, f32)], 9, 1,
    )(at, q_here, k_here, v_here, short_filter, decay, residues, skip_gain[None], norm_gain[None])
    sent, edge = call(
        edge_part, "edge_part", [(blocks, bf16), ((16 * GROUPS, LANES), f32)], [vmem((48 * GROUPS, LANES), f32)], 5,
    )(halo, heads, taps_t, rates, clean)
    near = lax.all_to_all(sent, "y", 0, 0, tiled=True)
    quads_out, total, step, before = call(
        scan_near, "scan_near", [(quads, bf16), (modes, bf16), (modes, f32), (modes, f32)], [], 3, 1,
    )(at, near, rates)
    total, upper_half, place = lax.optimization_barrier((total, at[0], at[1]))
    z = 4 * upper_half + place
    even = lax.rem(z, 2) == 0

    def swapped(first):
        return lambda t, _: lax.ppermute(t, Z, [(first, first + 1), (first + 1, first)]).astype(f32)

    def summed(mine, other):
        mine = mine.astype(f32)
        return step * jnp.where(even, mine, other) + jnp.where(even, other, mine)

    def by_pairs(total):
        other = lax.cond(z < 2, swapped(0), lambda _, o: o, total, step)
        pair = summed(total, other).astype(bf16)
        arrived = lax.ppermute(pair, Z, [(0, 2), (1, 3)])
        total, pair = lax.optimization_barrier((total, pair))
        other = lax.cond(z < 2, lambda _, o: o, swapped(2), total, other)
        arrived = arrived.astype(f32)
        four = (step * step * arrived + summed(total, other)).astype(bf16)
        return four, jnp.where(even, arrived, step * arrived + other)

    def unwritten(after, *outs):
        return call(lambda *_: None, "unwritten", outs, [], 1)(after)

    four, far = lax.cond(z < 4, by_pairs, lambda t: unwritten(t, (modes, bf16), (modes, f32)), total)
    carried = lax.ppermute(four, Z, [(2, 6), (3, 7)]), lax.ppermute(four, Z, [(2, 4), (3, 5)])
    quads_out, far, four = lax.optimization_barrier((quads_out, far, four))
    results = (natural, bf16), (natural, f32), ((8, LANES), f32)

    def finished(body, count, *own_args):
        return call(
            body, body.__name__, results,
            [vmem(modes, f32), vmem((16 * GROUPS, LANES), f32), vmem((ROWS, LANES), f32)],
            count, 1,
        )(at, *own_args, before, rates, weights, skip, qc, own, edge, residual, gain)

    def lower(_):
        done = finished(finish_lower, 11, far)
        return *done, *unwritten(far, (quads, bf16))

    def upper(_):
        quad = lax.all_to_all(quads_out, "place", 0, 0, tiled=True)
        return *unwritten(quad, *results), quad

    *done, quad = lax.cond(z < 4, lower, upper, 0)
    carried = carried[0] + carried[1]
    mixed, scaled, squares = lax.cond(
        z < 4, lambda d: d, lambda _: finished(finish_upper, 12, quad, carried), tuple(done)
    )
    gathered = lax.all_to_all(squares, "tensor", 0, 0, tiled=True)
    return call(
        normalise, "normalise", [(natural, bf16)] * 2, [vmem(natural, bf16), pltpu.SemaphoreType.DMA((3,))],
        3, far_out=True,
    )(mixed, scaled, gathered)


def solution(mesh):
    split = Mesh(mesh.devices.reshape(2, 4, 8, 8), CONTEXT + ("tensor",))
    rows = P(CONTEXT, "tensor")
    in_specs = (
        rows, rows, rows, P(None, None, "tensor"), P(None, "tensor"), P(None, "tensor"),
        P("tensor"), rows, P("tensor"),
    )
    return jax.shard_map(shards, mesh=split, in_specs=in_specs, out_specs=(rows, rows), check_vma=False)
```
